32 devices in a mesh: dp: 2 (over x), head: 16 (over z, y, core).
Axes of the slice: x: 2, y: 2, z: 4, core: 2. Of those that a mesh axis runs over, the one named last changes fastest.
Arguments:
- queries: bfloat16 [2048, 8192], P('dp', 'head'), may hold values from -14 to 14
- keys: bfloat16 [2048, 8192], P('dp', 'head'), may hold values from -14 to 14
- values: bfloat16 [2048, 8192], P('dp', 'head'), may hold values from -24 to 24
Outputs:
- regrouped: bfloat16 [2048, 8192], P(('dp', 'head'))
- hessian: float32 [8192, 8192], P('dp', 'head')
The draws below stay inside these ranges and needn't reach their ends.
All inputs are finite; a program needn't handle non-finite values.
Results may differ from the reference program's by a relative error of at most 0.0044.
Values may be sent and summed in bfloat16 or wider, within the bound.
A program may use at most 128 MiB of HBM per device.

```python
import math
import jax
import jax.numpy as jnp
from jax import lax

HEADS = 64
HEAD_SIZE = 128
D = 8192
LEN = 1024
TOKENS = 2048


def paired_fields(base_key):
    query_key, other_key = jax.random.split(base_key, 2)
    query_vals = jnp.clip(2.5 * jax.random.normal(query_key, (TOKENS, D), jnp.float32), -14.0, 14.0)
    key_vals = jnp.clip(2.5 * jax.random.normal(other_key, (TOKENS, D), jnp.float32), -14.0, 14.0)
    return (query_vals, key_vals)


def draw_queries(key, part):
    return paired_fields(jax.random.fold_in(key, 11))[0].astype(jnp.bfloat16)


def draw_keys(key, part):
    return paired_fields(jax.random.fold_in(key, 11))[1].astype(jnp.bfloat16)


def spiked(values, rng, source, target, shards_of, factor):
    def block_of(position):
        return (jnp.arange(values.shape[position]) // (values.shape[position] // shards_of)).reshape((-1,) + (1,) * (values.ndim - 1 - position))

    near = jax.random.permutation(rng, shards_of)[block_of(target)]
    other_side = (block_of(target) + shards_of // 2) % shards_of
    return jnp.where((block_of(source) == near) | (block_of(source) == other_side), factor * values, values)


def shard_levels(key, dims, pieces, smallest, high):
    def one(position, blocks):
        steps = jax.random.uniform(jax.random.fold_in(jax.random.fold_in(key, 6), position), (blocks,), jnp.float32, smallest / len(pieces), high / len(pieces))
        return jnp.repeat(jnp.exp(steps), dims[position] // blocks).reshape((-1,) + (1,) * (len(dims) - position - 1))

    factor_of = one(*pieces[0])
    for cut in pieces[1:]:
        factor_of = factor_of * one(*cut)
    return factor_of


def heavy_noise(stream_key, shape, deviation, bound, cuts, heavy, held_as=jnp.bfloat16):
    drawn = deviation * jax.random.normal(stream_key, shape, jnp.float32)
    if cuts:
        drawn = drawn * shard_levels(stream_key, shape, cuts, -0.22, 0.18)
    return jnp.clip(spiked(drawn, jax.random.fold_in(stream_key, 3), *heavy), -bound, bound).astype(held_as)


def setup_inputs(seed: int = 0) -> dict:
    key_of = jax.random.split(jax.random.key(seed), 4)
    return {
        "queries": draw_queries(jax.random.fold_in(key_of[3], 71), 0),
        "keys": draw_keys(jax.random.fold_in(key_of[3], 71), 0),
        "values": heavy_noise(key_of[2], (TOKENS, D), 4.0, 24.0, ((0, 2), (1, 16)), (0, 1, 16, 2.0)),
    }


def head_attention(operands):
    head_query_rows, head_key_rows, head_value_rows = operands
    logit_matrix = jnp.einsum('ixy,ijy->ixj', head_query_rows.astype(jnp.float32), head_key_rows.astype(jnp.float32)) * (1.0 / math.sqrt(HEAD_SIZE))
    causal = lax.broadcasted_iota(jnp.int32, (LEN, LEN), 0) >= lax.broadcasted_iota(jnp.int32, (LEN, LEN), 1)
    logit_matrix = jnp.where(causal[None], logit_matrix, -1e+30)
    peak = lax.optimization_barrier(jnp.max(logit_matrix, axis=-1, keepdims=True))
    raised = jnp.exp(logit_matrix - peak)
    attention_weight = (raised / lax.optimization_barrier(jnp.sum(raised, axis=-1, keepdims=True))).astype(jnp.bfloat16)
    attended_values = jnp.einsum('fjh,fhu->fju', attention_weight.astype(jnp.float32), head_value_rows.astype(jnp.float32))
    return attended_values.astype(jnp.bfloat16)

def reference(queries, keys, values):
    groups = TOKENS // LEN

    def split_heads(array):
        return jnp.transpose(array.reshape(groups, LEN, HEADS, HEAD_SIZE), (2, 0, 1, 3))
    outputs = lax.map(head_attention, (split_heads(queries), split_heads(keys), split_heads(values)))
    regrouped = jnp.transpose(outputs, (1, 2, 0, 3)).reshape(TOKENS, D)
    widened = regrouped.astype(jnp.float32)
    hessian = jnp.dot(widened.T, widened, precision=lax.Precision.HIGHEST) * (2.0 / TOKENS)
    return (regrouped, hessian)
```

```python
import functools
import math

import jax
import jax.numpy as jnp
from jax import lax
from jax.experimental import pallas as pl
from jax.experimental.pallas import tpu as pltpu
from jax.sharding import PartitionSpec as P

HEAD_SIZE = 128
MESH = pl.DeviceIdType.MESH


def exchange_kernel(
    groups, heads, scale,
    query_hbm, key_hbm, value_hbm, regrouped_ref, total,
    query_ref, key_ref, value_ref, gathered, leaving, arrived, lent, relayed,
    ring_send, ring_recv, pair_send, pair_recv, sum_send, sum_recv,
    rows_sem, load_sem, lent_send, lent_recv, relay_send,
):
    rows, cols = query_ref.shape
    half = rows // 2
    quarter = rows // 4
    chips = heads // 2
    depth = chips // 2
    per_group = heads // groups
    rows_out = rows // heads
    tile = min(cols, 256)
    me = lax.axis_index("dp")
    here = lax.axis_index("head")
    core = lax.rem(here, 2)
    chip = lax.div(here, 2)
    layers = chips // 2
    side = lax.rem(chip, 2)
    level = lax.div(chip, 2)
    place = level + side * (2 * layers - 1 - 2 * level)

    def head_at(position, which):
        spot = lax.rem(position + 2 * chips, chips)
        far = lax.div(spot, layers)
        height = spot + far * (2 * layers - 1 - 2 * spot)
        return (height * 2 + far) * 2 + which

    right = head_at(place + 1, core)
    left = head_at(place - 1, core)
    partner = here + 1 - 2 * core

    loads = [
        pltpu.make_async_copy(source, target, load_sem.at[n])
        for n, (source, target) in enumerate(
            ((query_hbm, query_ref), (key_hbm, key_ref), (value_hbm, value_ref))
        )
    ]
    for load in loads:
        load.start()
    lending = groups == 2 and layers >= 4
    lends = level == (layers - 1) * me
    borrows = level == (layers - 1) * (1 - me)
    held = (level + 2 * me - 1) * 2 + 1 - side
    mirror = ((layers - 1 - level) * 2 + side) * 2 + core

    barrier = pltpu.get_barrier_semaphore()
    if lending:
        pl.semaphore_signal(barrier, inc=1, device_id=(me, mirror), device_id_type=MESH)
    for other in (right, left, partner):
        pl.semaphore_signal(barrier, inc=1, device_id=(me, other), device_id_type=MESH)
    for shift in range(1, groups):
        pl.semaphore_signal(
            barrier, inc=1, device_id=(lax.rem(me + shift, groups), here), device_id_type=MESH
        )

    def attend(part):
        def head_of(index, carry):
            lanes = pl.ds(pl.multiple_of(index * HEAD_SIZE, HEAD_SIZE), HEAD_SIZE)
            for strip in range(2 * part, 2 * part + 2):
                seen = (strip + 1) * quarter
                here_rows = pl.ds(strip * quarter, quarter)
                logits = lax.dot_general(
                    query_ref[here_rows, lanes], key_ref[pl.ds(0, seen), lanes],
                    (((1,), (1,)), ((), ())), preferred_element_type=jnp.float32,
                ) * (1.0 / math.sqrt(HEAD_SIZE))
                row = lax.broadcasted_iota(jnp.int32, logits.shape, 0) + strip * quarter
                column = lax.broadcasted_iota(jnp.int32, logits.shape, 1)
                logits = jnp.where(row >= column, logits, -1e30)
                raised = jnp.exp(logits - jnp.max(logits, axis=-1, keepdims=True))
                weight = raised * (1.0 / jnp.sum(raised, axis=-1, keepdims=True))
                gathered[here, here_rows, lanes] = jnp.dot(
                    weight.astype(jnp.bfloat16), value_ref[pl.ds(0, seen), lanes],
                    preferred_element_type=jnp.float32,
                ).astype(jnp.bfloat16)
            return carry

        lax.fori_loop(0, cols // HEAD_SIZE, head_of, 0)

    def block(head, part):
        return gathered.at[head, pl.ds(part * half, half)]

    def ring(direction, part, step):
        source = head_at(place + step * (2 * direction - 1), core)
        ref = block(source, part)
        return pltpu.make_async_remote_copy(
            src_ref=ref, dst_ref=ref,
            send_sem=ring_send.at[direction, part, step],
            recv_sem=ring_recv.at[direction, part, step],
            device_id=(me, right if direction == 0 else left), device_id_type=MESH,
        )

    def ring_arrival(direction, part, step):
        source = head_at(place + step * (2 * direction - 1), core)
        ref = block(source, part)
        return pltpu.make_async_remote_copy(
            src_ref=ref, dst_ref=ref,
            send_sem=ring_send.at[direction, part, step - 1],
            recv_sem=ring_recv.at[direction, part, step - 1],
            device_id=(me, right if direction == 0 else left), device_id_type=MESH,
        )

    def pair(direction, part, step, which):
        ref = block(head_at(place + step * (2 * direction - 1), which), part)
        return pltpu.make_async_remote_copy(
            src_ref=ref, dst_ref=ref,
            send_sem=pair_send.at[direction, part, step],
            recv_sem=pair_recv.at[direction, part, step],
            device_id=(me, partner), device_id_type=MESH,
        )

    def sum_copy(shift, local):
        return pltpu.make_async_remote_copy(
            src_ref=leaving.at[shift - 1, local], dst_ref=arrived.at[shift - 1, local],
            send_sem=sum_send.at[shift - 1, local], recv_sem=sum_recv.at[shift - 1, local],
            device_id=(lax.rem(me + shift, groups), here), device_id_type=MESH,
        )

    def rows_copy(head):
        return pltpu.make_async_copy(
            gathered.at[head, pl.ds(pl.multiple_of(here * rows_out, rows_out), rows_out)],
            regrouped_ref.at[:, pl.ds(pl.multiple_of(head * cols, cols), cols)],
            rows_sem.at[head],
        )

    def gram(head):
        rows_copy(head).start()
        owner = lax.div(head, per_group)
        local = lax.rem(head, per_group)
        shift = lax.rem(owner - me + groups, groups)

        def one(t, carry):
            where = pl.ds(pl.multiple_of(t * tile, tile), tile)
            term = lax.dot_general(
                gathered[head, :, where], gathered[here],
                (((0,), (0,)), ((), ())), preferred_element_type=jnp.float32,
            )

            @pl.when(shift == 0)
            def _():
                total[local, where] = term

            @pl.when(shift != 0)
            def _():
                leaving[shift - 1, local, where] = term.astype(jnp.bfloat16)

            return carry

        lax.fori_loop(0, cols // tile, one, 0)

        sends = shift != 0
        if lending:
            sends = sends & jnp.logical_not(borrows & (lax.div(head, 2) == held))

        @pl.when(sends)
        def _():
            sum_copy(shift, local).start()

    def lent_copy(which):
        return pltpu.make_async_remote_copy(
            src_ref=lent.at[which], dst_ref=relayed.at[which],
            send_sem=lent_send.at[which], recv_sem=lent_recv.at[which],
            device_id=(1 - me, here), device_id_type=MESH,
        )

    def relay_copy(which):
        local = lax.rem((level * 2 + 1 - side) * 2 + which, per_group)
        return pltpu.make_async_remote_copy(
            src_ref=relayed.at[which], dst_ref=arrived.at[0, local],
            send_sem=relay_send.at[which], recv_sem=sum_recv.at[0, local],
            device_id=(me, mirror), device_id_type=MESH,
        )

    def gram_for_mirror(which):
        head = (level * 2 + 1 - side) * 2 + which

        def one(t, carry):
            where = pl.ds(pl.multiple_of(t * tile, tile), tile)
            lent[which, where] = lax.dot_general(
                gathered[head, :, where], gathered[mirror],
                (((0,), (0,)), ((), ())), preferred_element_type=jnp.float32,
            ).astype(jnp.bfloat16)
            return carry

        lax.fori_loop(0, cols // tile, one, 0)
        lent_copy(which).start()

    def gram_far(head):
        if not lending:
            gram(head)
            return

        @pl.when(lends)
        def _():
            rows_copy(head).start()

        @pl.when(jnp.logical_not(lends))
        def _():
            gram(head)

    reach = {(0, 0): depth, (1, 0): depth - 1, (0, 1): depth - 1, (1, 1): depth}
    for load in loads:
        load.wait()
    for part in range(2):
        attend(part)
        if part == 0:
            pl.semaphore_wait(barrier, 3 + groups - 1 + int(lending))
        for direction in range(2):
            ring(direction, part, 0).start()
        pair(0, part, 0, core).start()
    gram(here)

    def receive(part, step):
        for direction in range(2):
            ring_arrival(direction, part, step).wait_recv()
            if reach[direction, part] == depth:
                ring(direction, part, step).start()
            else:
                @pl.when(step < depth - 1)
                def _():
                    ring(direction, part, step).start()
            pair(direction, part, step, core).start()

    def pair_arrivals(step):
        for part in range(2):
            for direction in range(2):
                pair(direction, part, step, 1 - core).wait_recv()

    def advance(step, carry):
        receive(0, step)

        @pl.when(step == 1)
        def _():
            for part in range(2):
                pair(0, part, 0, 1 - core).wait_recv()
            gram(partner)

        @pl.when(step > 1)
        def _():
            pair_arrivals(step - 1)
            gram(head_at(place - step + 1, 1 - core))
            gram(head_at(place + step - 1, 1 - core))

        receive(1, step)
        if lending:
            @pl.when(borrows & (step == depth - 1))
            def _():
                for which in range(2):
                    gram_for_mirror(which)
                for which in range(2):
                    sum_copy(1, lax.rem(held * 2 + which, per_group)).start()

        gram(head_at(place - step, core))
        gram(head_at(place + step, core))
        return carry

    lax.fori_loop(1, depth, advance, 0)
    for direction, part in ((0, 0), (1, 1)):
        ring_arrival(direction, part, depth).wait_recv()
        pair(direction, part, depth, core).start()
    if depth > 1:
        pair_arrivals(depth - 1)
        gram(head_at(place - depth + 1, 1 - core))
        gram(head_at(place + depth - 1, 1 - core))
    gram_far(head_at(place - depth, core))
    for direction, part in ((0, 0), (1, 1)):
        pair(direction, part, depth, 1 - core).wait_recv()
    gram_far(head_at(place - depth, 1 - core))

    def finish(order, carry):
        if lending:
            @pl.when(lends & (order == 4))
            def _():
                for which in range(2):
                    lent_copy(which).wait_recv()
                    relay_copy(which).start()

        away = lax.div(order, 4)
        kind = lax.rem(order, 4)
        head = head_at(
            place + (away + 1) * (2 * lax.rem(kind, 2) - 1), lax.rem(core + lax.div(kind, 2), 2)
        )
        collect(head)
        return carry

    def collect(head):
        owner = lax.div(head, per_group)
        local = lax.rem(head, per_group)

        @pl.when(owner == me)
        def _():
            for shift in range(1, groups):
                sum_copy(shift, local).wait_recv()
            value = total[local]
            for shift in range(1, groups):
                value = value + arrived[shift - 1, local].astype(jnp.float32)
            total[local] = value * scale

    collect(here)
    collect(partner)
    lax.fori_loop(0, 4 * (depth - 1), finish, 0)
    collect(head_at(place - depth, core))
    collect(head_at(place - depth, 1 - core))

    if lending:
        @pl.when(lends)
        def _():
            for which in range(2):
                relay_copy(which).wait_send()

    def drain(head, carry):
        rows_copy(head).wait()
        owner = lax.div(head, per_group)
        local = lax.rem(head, per_group)
        shift = lax.rem(owner - me + groups, groups)

        sends = shift != 0
        if lending:
            lent_out = lends & (lax.div(head, 2) == (layers - 1 - level) * 2 + 1 - side)
            sends = sends & jnp.logical_not(lent_out)

        @pl.when(sends)
        def _():
            sum_copy(shift, local).wait_send()

        return carry

    lax.fori_loop(0, heads, drain, 0)

    def drain_sends(step, carry):
        for (direction, part), distance in reach.items():
            @pl.when(step < distance)
            def _():
                ring(direction, part, step).wait_send()

            @pl.when((step > 0) & (step <= distance))
            def _():
                pair(direction, part, step, core).wait_send()
        return carry

    lax.fori_loop(0, depth + 1, drain_sends, 0)
    for part in range(2):
        pair(0, part, 0, core).wait_send()
    if lending:
        @pl.when(borrows)
        def _():
            for which in range(2):
                lent_copy(which).wait_send()


def exchange(queries, keys, values, groups, heads):
    rows, cols = queries.shape
    per_group = heads // groups
    depth = heads // 4
    dma = pltpu.SemaphoreType.DMA
    vmem = pl.BlockSpec(memory_space=pltpu.VMEM)
    return pl.pallas_call(
        functools.partial(exchange_kernel, groups, heads, 2.0 / (rows * groups)),
        out_shape=(
            pltpu.VMEM((rows // heads, heads * cols), jnp.bfloat16),
            pltpu.VMEM((per_group, cols, cols), jnp.float32),
        ),
        in_specs=[pl.BlockSpec(memory_space=pltpu.HBM)] * 3,
        out_specs=(vmem, vmem),
        scratch_shapes=[
            pltpu.VMEM((rows, cols), jnp.bfloat16),
            pltpu.VMEM((rows, cols), jnp.bfloat16),
            pltpu.VMEM((rows, cols), jnp.bfloat16),
            pltpu.VMEM((heads, rows, cols), jnp.bfloat16),
            pltpu.VMEM((groups - 1, per_group, cols, cols), jnp.bfloat16),
            pltpu.VMEM((groups - 1, per_group, cols, cols), jnp.bfloat16),
            pltpu.VMEM((2, cols, cols), jnp.bfloat16),
            pltpu.VMEM((2, cols, cols), jnp.bfloat16),
            dma((2, 2, depth)),
            dma((2, 2, depth)),
            dma((2, 2, depth + 1)),
            dma((2, 2, depth + 1)),
            dma((groups - 1, per_group)),
            dma((groups - 1, per_group)),
            dma((heads,)),
            dma((3,)),
            dma((2,)),
            dma((2,)),
            dma((2,)),
        ],
        compiler_params=pltpu.CompilerParams(
            collective_id=0, has_side_effects=True, vmem_limit_bytes=109 * 512 * 1024
        ),
    )(queries, keys, values)


LAYERS = 4
RECV, SEND, GRAM, ROWS, HELD, MAKE, TAKE, IDLE = range(8)
OPS = (
    (
        14848, 14976, 8448, 9088, 33282, 33410, 49666, 49794, 2305, 4353, 8200, 8208, 8256, 33290, 33298,
        770, 898, 17154, 49674, 49682, 17282, 2433, 8840, 12432, 8384, 33418, 33426, 66, 194, 16450, 49802,
        49810, 16578, 769, 4481, 8456, 34848, 8264, 778, 74, 17162, 16458, 4113, 8344, 34976, 8904, 33434,
        202, 49818, 16586, 521, 8584, 34864, 12624, 906, 17290, 4145, 8216, 35232, 9024, 33306, 49690, 777,
        8536, 39216, 8400, 210, 16594, 4305, 34872, 8464, 8520, 786, 17170, 35640, 33056, 8272, 4643, 68131,
        137763, 82, 16466, 2337, 8408, 37296, 8648, 218, 4369, 16602, 8592, 8640, 914, 322, 450, 16706, 330,
        458, 16714, 16842, 338, 16722, 346, 35768, 16730, 17298, 16834, 2481, 32944, 12752, 201267, 466,
        16850, 8472, 794, 2225, 17178, 8280, 90, 33464, 266811, 16474, 8664, 474, 16858, 8600, 922, 17306,
        16420, 44, 16428, 16436, 16444,
    ),
    (
        15888, 11408, 13072, 8592, 33298, 33426, 49682, 49810, 4241, 2321, 8704, 8216, 33824, 8272, 33282,
        33306, 786, 914, 17170, 49666, 49690, 17298, 4177, 2449, 8832, 8472, 33952, 8528, 33410, 794, 49794,
        17178, 4497, 9088, 8344, 35888, 8256, 898, 33434, 17282, 49818, 2209, 665, 8328, 8280, 34208, 12752,
        33418, 338, 466, 16722, 49802, 16850, 8960, 8600, 36144, 12496, 770, 922, 66, 16450, 82, 210, 16466,
        90, 16474, 17154, 17306, 16594, 1297, 921, 8392, 8664, 35248, 12736, 450, 202, 474, 16834, 16586,
        16858, 2465, 8712, 8408, 34080, 8384, 4643, 68131, 137763, 33290, 194, 218, 49674, 16578, 16602,
        713, 1457, 2337, 8512, 8648, 8264, 8520, 322, 74, 330, 458, 16706, 16458, 16714, 16842, 1425, 8456,
        8584, 8536, 778, 906, 346, 17162, 17290, 16730, 36016, 201267, 264755, 334387, 2360, 1113, 1433,
        440, 184, 16420, 44, 16428, 16436, 60, 16444,
    ),
    (
        3616, 1184, 6944, 416, 12816, 96, 35888, 33298, 4643, 68131, 137763, 49682, 1441, 2465, 296, 13072,
        224, 32944, 786, 17170, 673, 2209, 8216, 33306, 8192, 352, 34096, 33282, 49690, 49666, 8472, 794,
        8832, 480, 36272, 201267, 33410, 17178, 49794, 1313, 2225, 13184, 12352, 32952, 898, 66, 17282,
        16450, 929, 8344, 8400, 35128, 33434, 32978, 9288, 32842, 49818, 49362, 49226, 2345, 8960, 8512,
        12368, 4249, 770, 322, 82, 9608, 33674, 17154, 16706, 16466, 50058, 1201, 537, 12696, 8640, 33208,
        922, 450, 8280, 90, 17306, 16834, 16474, 8712, 8656, 8408, 522, 466, 218, 8336, 658, 16906, 16850,
        16602, 17042, 8904, 12624, 8328, 4545, 650, 202, 338, 8592, 914, 17034, 16586, 16722, 17298, 913,
        8664, 474, 8536, 8384, 194, 346, 16858, 16578, 16730, 665, 8456, 778, 8648, 8520, 330, 458, 17162,
        16714, 16842, 657, 32824, 266811, 16420, 44, 16428, 16436, 16444,
    ),
    (
        7216, 7344, 304, 432, 1329, 4401, 112, 32800, 34872, 4659, 1457, 4529, 240, 33056, 35000, 2337,
        1209, 368, 8208, 33080, 33298, 49682, 2353, 1337, 496, 12560, 33208, 70203, 786, 17170, 13392,
        34976, 82, 8472, 33562, 16466, 49946, 2361, 1465, 12496, 12416, 33410, 32978, 8280, 90, 49794,
        49362, 16474, 2081, 8256, 8576, 898, 32834, 9432, 32986, 17282, 49218, 49370, 2489, 12752, 33184,
        135715, 199203, 268835, 466, 9352, 33418, 16850, 49802, 2481, 8512, 12544, 770, 322, 9688, 474,
        17154, 16706, 16858, 2465, 8264, 8216, 4481, 538, 32842, 9480, 778, 16922, 49226, 17162, 1081, 8520,
        12296, 522, 330, 16906, 16714, 8584, 906, 12624, 10440, 202, 338, 17290, 16586, 16722, 8192, 514,
        8648, 12688, 914, 458, 16898, 17298, 16842, 8536, 346, 8640, 8344, 666, 450, 16730, 17050, 16834,
        8600, 922, 8384, 8336, 658, 194, 17306, 17042, 16578, 16420, 44, 16428, 16436, 16444,
    ),
)
MADE = 8


def routed_kernel(
    heads, scale,
    query_hbm, key_hbm, value_hbm, regrouped_ref, total,
    query_ref, key_ref, value_ref, store, made, taken, landed,
    recv_sem, send_sem, made_sem, take_sem, rows_send, rows_recv, load_sem,
):
    rows, cols = query_ref.shape
    quarter = rows // 4
    half = rows // 2
    wide = cols // 2
    rows_out = rows // heads
    layer = heads // LAYERS
    me = lax.axis_index("dp")
    here = lax.axis_index("head")
    core = lax.rem(here, 2)
    chip = lax.div(here, 2)
    side = lax.rem(chip, 2)
    level = lax.div(chip, 2)
    role = level + me * (LAYERS - 1 - 2 * level)
    up = (1 - 2 * me) * layer
    across = 2 - 4 * side
    cross = 1 - 2 * core
    mine = (me * heads + here) * 4
    channels = {
        0: (me, here + up), 1: (me, here - up), 2: (1 - me, here),
        3: (me, here + across), 4: (me, here + cross),
    }

    loads = []
    for strip in range(4):
        part = pl.ds(strip * quarter, quarter)
        group = [
            pltpu.make_async_copy(source.at[part], target.at[part], load_sem.at[strip * 3 + n])
            for n, (source, target) in enumerate(
                ((query_hbm, query_ref), (key_hbm, key_ref), (value_hbm, value_ref))
            )
        ]
        for load in group:
            load.start()
        loads.append(group)

    barrier = pltpu.get_barrier_semaphore()
    for rise in (-1, 0, 1):
        @pl.when((role + rise >= 0) & (role + rise < LAYERS))
        def _():
            for turn in range(2):
                for swap in range(2):
                    if (rise, turn, swap) == (0, 0, 0):
                        continue
                    there = here + rise * up + turn * across + swap * cross
                    pl.semaphore_signal(barrier, inc=1, device_id=(me, there), device_id_type=MESH)
    pl.semaphore_signal(barrier, inc=1, device_id=(1 - me, here), device_id_type=MESH)
    ends = lax.rem(lax.div(role + 1, 2) + 1, 2)

    def base_of(block):
        other = lax.div(block, 8)
        height = lax.rem(lax.div(block, 2), 4)
        turn = lax.rem(block, 2)
        sequence = me + other - 2 * me * other
        floor = height + me * (LAYERS - 1 - 2 * height)
        spot = floor * 2 + side + turn - 2 * side * turn
        return (sequence * heads + spot * 2 + core) * 4

    length = max(len(ops) for ops in OPS)

    def pick(index):
        words = [ops[index] if index < len(ops) else IDLE for ops in OPS]
        low = jnp.where(role == 0, words[0], words[1])
        high = jnp.where(role == 2, words[2], words[3])
        return jnp.where(role < 2, low, high)

    def word_at(index, first, last):
        if last - first == 1:
            return pick(first)
        middle = (first + last) // 2
        return lax.cond(
            index < middle, lambda: word_at(index, first, middle), lambda: word_at(index, middle, last)
        )

    def copy(channel, slot):
        return pltpu.make_async_remote_copy(
            src_ref=store.at[slot], dst_ref=store.at[slot],
            send_sem=send_sem.at[channel], recv_sem=recv_sem.at[slot],
            device_id=channels[channel], device_id_type=MESH,
        )

    def send(mask, slot):
        for channel in range(5):
            @pl.when(lax.rem(lax.div(mask, 2 ** channel), 2) == 1)
            def _():
                copy(channel, slot).start()

    def head_of(slot):
        return lax.rem(lax.div(slot, 4), heads)

    def columns(head, pair):
        return pl.ds(pl.multiple_of(head * cols + pair * wide, wide), wide)

    def keep_rows(slot):
        first = here * rows_out - lax.rem(lax.div(slot, 2), 2) * half

        @pl.when((first >= 0) & (first < half))
        def _():
            regrouped_ref[:, columns(head_of(slot), lax.rem(slot, 2))] = store[
                slot, pl.ds(pl.multiple_of(first, rows_out), rows_out)
            ]

    def rows_copy(base, mask, number, pair):
        there = here + (lax.rem(mask, 4) - 1) * up + lax.rem(lax.div(mask, 4), 2) * across
        there = there + lax.div(mask, 8) * cross
        late = lax.div(there * rows_out, half)
        return pltpu.make_async_remote_copy(
            src_ref=store.at[
                base + late * 2 + pair,
                pl.ds(pl.multiple_of(there * rows_out - late * half, rows_out), rows_out),
            ],
            dst_ref=landed.at[head_of(base) * 2 + pair],
            send_sem=rows_send.at[number * 2 + pair], recv_sem=rows_recv.at[head_of(base) * 2 + pair],
            device_id=(me, there), device_id_type=MESH,
        )

    def take_copy(channel, number):
        return pltpu.make_async_remote_copy(
            src_ref=made.at[number], dst_ref=taken.at[number],
            send_sem=made_sem.at[number], recv_sem=take_sem.at[number],
            device_id=channels[channel], device_id_type=MESH,
        )

    def local_rows(slot, pair):
        return pl.ds(pl.multiple_of((head_of(slot) - me * (heads // 2)) * cols + pair * wide, wide), wide)

    def term(left, right):
        return lax.dot_general(
            store[left], store[right], (((0,), (0,)), ((), ())), preferred_element_type=jnp.float32,
        )

    def attend(strip, pair):
        seen = (strip + 1) * quarter
        here_rows = pl.ds(strip * quarter, quarter)
        for inner in range(wide // HEAD_SIZE):
            lanes = pl.ds(pl.multiple_of(pair * wide + inner * HEAD_SIZE, HEAD_SIZE), HEAD_SIZE)
            logits = lax.dot_general(
                query_ref[here_rows, lanes], key_ref[pl.ds(0, seen), lanes],
                (((1,), (1,)), ((), ())), preferred_element_type=jnp.float32,
            ) * (1.0 / math.sqrt(HEAD_SIZE))
            row = lax.broadcasted_iota(jnp.int32, logits.shape, 0) + strip * quarter
            column = lax.broadcasted_iota(jnp.int32, logits.shape, 1)
            logits = jnp.where(row >= column, logits, -1e30)
            raised = jnp.exp(logits - jnp.max(logits, axis=-1, keepdims=True))
            weight = raised * (1.0 / jnp.sum(raised, axis=-1, keepdims=True))
            store[
                mine + strip // 2 * 2 + pair, pl.ds(strip % 2 * quarter, quarter),
                pl.ds(inner * HEAD_SIZE, HEAD_SIZE),
            ] = jnp.dot(
                weight.astype(jnp.bfloat16), value_ref[pl.ds(0, seen), lanes],
                preferred_element_type=jnp.float32,
            ).astype(jnp.bfloat16)

    for part in range(2):
        for strip in ((0, 1, 2, 3) if part == 0 else ()):
            for load in loads[strip]:
                load.wait()

        def of_pair(pair, carry):
            for strip in (2 * part, 2 * part + 1):
                attend(strip, pair)
            if part == 0:
                @pl.when(pair == 0)
                def _():
                    pl.semaphore_wait(barrier, 3 * layer - ends * layer)
            piece = part * 2 + pair
            send(lax.rem(lax.div(word_at(piece, 0, 4), 512), 32), mine + piece)
            keep_rows(mine + piece)
            return carry

        lax.fori_loop(0, 2, of_pair, 0)

    def step(index, carry):
        word = word_at(index, 4, length)
        kind = lax.rem(word, 8)
        base = base_of(lax.rem(lax.div(word, 8), 16))
        piece = lax.rem(lax.div(word, 128), 4)
        mask = lax.rem(lax.div(word, 512), 32)
        lane = lax.rem(lax.div(word, 16384), 2)
        flag = lax.rem(lax.div(word, 32768), 2)
        number = lax.div(word, 65536)
        base = base + lane * cross * 4
        slot = base + piece

        @pl.when(kind <= SEND)
        def _():
            @pl.when(kind == RECV)
            def _():
                copy(4, slot).wait_recv()
            send(mask, slot)

            @pl.when(flag == 1)
            def _():
                keep_rows(slot)

        @pl.when(kind == GRAM)
        def _():
            @pl.when(lane == 1)
            def _():
                copy(4, slot).wait_recv()
            own = (lax.div(slot, heads * 4) * heads + here) * 4 + lax.div(piece, 2) * 2
            target = local_rows(slot, lax.rem(piece, 2))
            for other in range(2):
                lanes = pl.ds(other * wide, wide)
                total[target, lanes] = (
                    jnp.where(flag == 1, 0.0, total[target, lanes]) + term(slot, own + other) * scale
                )

            @pl.when(mask == 1)
            def _():
                keep_rows(slot)

        @pl.when((kind > GRAM) & (kind != IDLE))
        def _():
            @pl.when(kind == ROWS)
            def _():
                for pair in range(2):
                    rows_copy(base, mask, number, pair).start()

            @pl.when(kind == HELD)
            def _():
                for pair in range(2):
                    pltpu.make_async_remote_copy(
                        src_ref=store.at[base, pl.ds(0, rows_out)],
                        dst_ref=landed.at[head_of(base) * 2 + pair],
                        send_sem=rows_send.at[pair], recv_sem=rows_recv.at[head_of(base) * 2 + pair],
                        device_id=channels[4], device_id_type=MESH,
                    ).wait_recv()
                    regrouped_ref[:, columns(head_of(base), pair)] = landed[head_of(base) * 2 + pair]

            @pl.when(kind == MAKE)
            def _():
                column = base_of(lax.div(number, 16))
                far = lax.rem(base + 4 * heads, 8 * heads)
                column_far = lax.rem(column + 4 * heads, 8 * heads)
                for other in range(2):
                    value = jnp.zeros((wide, wide), jnp.float32)
                    for left, right in ((base, column), (far, column_far)):
                        for part in range(2):
                            value = value + term(left + part * 2 + piece, right + part * 2 + other)
                    made[lax.rem(number, 16), :, other * wide:(other + 1) * wide] = value.astype(jnp.bfloat16)
                for channel in range(4):
                    @pl.when(lax.rem(lax.div(mask, 2 ** channel), 2) == 1)
                    def _():
                        take_copy(channel, lax.rem(number, 16)).start()

            @pl.when(kind == TAKE)
            def _():
                take_copy(0, number).wait_recv()
                total[local_rows(base, piece), :] = taken[number].astype(jnp.float32) * scale

        return carry

    lax.fori_loop(4, length, step, 0)

    for which, ops in enumerate(OPS):
        @pl.when(role == which)
        def _():
            for channel in range(5):
                count = sum(word & 7 <= SEND and word >> 9 + channel & 1 for word in ops)
                if count:
                    sent = store.at[pl.ds(0, count)]
                    pltpu.make_async_remote_copy(
                        src_ref=sent, dst_ref=sent, send_sem=send_sem.at[channel],
                        recv_sem=recv_sem.at[0], device_id=channels[4], device_id_type=MESH,
                    ).wait_send()
            for word in ops:
                if word & 7 == ROWS:
                    for pair in range(2):
                        rows_copy(base_of(word >> 3 & 15), word >> 9 & 31, word >> 16, pair).wait_send()
                if word & 7 == MAKE:
                    take_copy(4, word >> 16 & 15).wait_send()


def routed(queries, keys, values, groups, heads):
    rows, cols = queries.shape
    dma = pltpu.SemaphoreType.DMA
    vmem = pl.BlockSpec(memory_space=pltpu.VMEM)
    shard = pltpu.VMEM((rows, cols), jnp.bfloat16)
    strip = pltpu.VMEM((MADE, cols // 2, cols), jnp.bfloat16)
    return pl.pallas_call(
        functools.partial(routed_kernel, heads, 2.0 / (rows * groups)),
        out_shape=(
            pltpu.VMEM((rows // heads, heads * cols), jnp.bfloat16),
            pltpu.VMEM((heads // groups * cols, cols), jnp.float32),
        ),
        in_specs=[pl.BlockSpec(memory_space=pltpu.HBM)] * 3,
        out_specs=(vmem, vmem),
        scratch_shapes=[
            shard, shard, shard,
            pltpu.VMEM((groups * heads * 4, rows // 2, cols // 2), jnp.bfloat16),
            strip, strip,
            pltpu.VMEM((heads * 2, rows // heads, cols // 2), jnp.bfloat16),
            dma((groups * heads * 4,)),
            dma((5,)),
            dma((MADE,)),
            dma((MADE,)),
            dma((heads * 2,)),
            dma((heads * 2,)),
            dma((12,)),
        ],
        compiler_params=pltpu.CompilerParams(
            collective_id=0, has_side_effects=True, vmem_limit_bytes=109 * 512 * 1024
        ),
    )(queries, keys, values)


def body(queries, keys, values):
    cols = queries.shape[1]
    groups, heads = lax.axis_size("dp"), lax.axis_size("head")
    fits = groups == 2 and heads == 4 * LAYERS and cols % (4 * HEAD_SIZE) == 0
    regrouped, total = (routed if fits else exchange)(queries, keys, values, groups, heads)
    return (regrouped, total.reshape(-1, cols))


def solution(mesh):
    in_specs = (P("dp", "head"), P("dp", "head"), P("dp", "head"))
    out_specs = (P(("dp", "head"), None), P("dp", "head"))
    return jax.shard_map(body, mesh=mesh, in_specs=in_specs, out_specs=out_specs, check_vma=False)
```

```python
import functools
import math

import jax
import jax.numpy as jnp
from jax import lax
from jax.experimental import pallas as pl
from jax.experimental.pallas import tpu as pltpu
from jax.sharding import PartitionSpec as P

HEAD_SIZE = 128
MESH = pl.DeviceIdType.MESH


def exchange_kernel(
    groups, heads, scale,
    query_hbm, key_hbm, value_hbm, regrouped_ref, total,
    query_ref, key_ref, value_ref, gathered, leaving, arrived, lent, relayed,
    ring_send, ring_recv, pair_send, pair_recv, sum_send, sum_recv,
    rows_sem, load_sem, lent_send, lent_recv, relay_send,
):
    rows, cols = query_ref.shape
    half = rows // 2
    quarter = rows // 4
    chips = heads // 2
    depth = chips // 2
    per_group = heads // groups
    rows_out = rows // heads
    tile = min(cols, 256)
    me = lax.axis_index("dp")
    here = lax.axis_index("head")
    core = lax.rem(here, 2)
    chip = lax.div(here, 2)
    layers = chips // 2
    side = lax.rem(chip, 2)
    level = lax.div(chip, 2)
    place = level + side * (2 * layers - 1 - 2 * level)

    def head_at(position, which):
        spot = lax.rem(position + 2 * chips, chips)
        far = lax.div(spot, layers)
        height = spot + far * (2 * layers - 1 - 2 * spot)
        return (height * 2 + far) * 2 + which

    right = head_at(place + 1, core)
    left = head_at(place - 1, core)
    partner = here + 1 - 2 * core

    loads = [
        pltpu.make_async_copy(source, target, load_sem.at[n])
        for n, (source, target) in enumerate(
            ((query_hbm, query_ref), (key_hbm, key_ref), (value_hbm, value_ref))
        )
    ]
    for load in loads:
        load.start()
    lending = groups == 2 and layers >= 4
    lends = level == (layers - 1) * me
    borrows = level == (layers - 1) * (1 - me)
    held = (level + 2 * me - 1) * 2 + 1 - side
    mirror = ((layers - 1 - level) * 2 + side) * 2 + core

    barrier = pltpu.get_barrier_semaphore()
    if lending:
        pl.semaphore_signal(barrier, inc=1, device_id=(me, mirror), device_id_type=MESH)
    for other in (right, left, partner):
        pl.semaphore_signal(barrier, inc=1, device_id=(me, other), device_id_type=MESH)
    for shift in range(1, groups):
        pl.semaphore_signal(
            barrier, inc=1, device_id=(lax.rem(me + shift, groups), here), device_id_type=MESH
        )

    def attend(part):
        def head_of(index, carry):
            lanes = pl.ds(pl.multiple_of(index * HEAD_SIZE, HEAD_SIZE), HEAD_SIZE)
            for strip in range(2 * part, 2 * part + 2):
                seen = (strip + 1) * quarter
                here_rows = pl.ds(strip * quarter, quarter)
                logits = lax.dot_general(
                    query_ref[here_rows, lanes], key_ref[pl.ds(0, seen), lanes],
                    (((1,), (1,)), ((), ())), preferred_element_type=jnp.float32,
                ) * (1.0 / math.sqrt(HEAD_SIZE))
                row = lax.broadcasted_iota(jnp.int32, logits.shape, 0) + strip * quarter
                column = lax.broadcasted_iota(jnp.int32, logits.shape, 1)
                logits = jnp.where(row >= column, logits, -1e30)
                raised = jnp.exp(logits - jnp.max(logits, axis=-1, keepdims=True))
                weight = raised * (1.0 / jnp.sum(raised, axis=-1, keepdims=True))
                gathered[here, here_rows, lanes] = jnp.dot(
                    weight.astype(jnp.bfloat16), value_ref[pl.ds(0, seen), lanes],
                    preferred_element_type=jnp.float32,
                ).astype(jnp.bfloat16)
            return carry

        lax.fori_loop(0, cols // HEAD_SIZE, head_of, 0)

    def block(head, part):
        return gathered.at[head, pl.ds(part * half, half)]

    def ring(direction, part, step):
        source = head_at(place + step * (2 * direction - 1), core)
        ref = block(source, part)
        return pltpu.make_async_remote_copy(
            src_ref=ref, dst_ref=ref,
            send_sem=ring_send.at[direction, part, step],
            recv_sem=ring_recv.at[direction, part, step],
            device_id=(me, right if direction == 0 else left), device_id_type=MESH,
        )

    def ring_arrival(direction, part, step):
        source = head_at(place + step * (2 * direction - 1), core)
        ref = block(source, part)
        return pltpu.make_async_remote_copy(
            src_ref=ref, dst_ref=ref,
            send_sem=ring_send.at[direction, part, step - 1],
            recv_sem=ring_recv.at[direction, part, step - 1],
            device_id=(me, right if direction == 0 else left), device_id_type=MESH,
        )

    def pair(direction, part, step, which):
        ref = block(head_at(place + step * (2 * direction - 1), which), part)
        return pltpu.make_async_remote_copy(
            src_ref=ref, dst_ref=ref,
            send_sem=pair_send.at[direction, part, step],
            recv_sem=pair_recv.at[direction, part, step],
            device_id=(me, partner), device_id_type=MESH,
        )

    def sum_copy(shift, local):
        return pltpu.make_async_remote_copy(
            src_ref=leaving.at[shift - 1, local], dst_ref=arrived.at[shift - 1, local],
            send_sem=sum_send.at[shift - 1, local], recv_sem=sum_recv.at[shift - 1, local],
            device_id=(lax.rem(me + shift, groups), here), device_id_type=MESH,
        )

    def rows_copy(head):
        return pltpu.make_async_copy(
            gathered.at[head, pl.ds(pl.multiple_of(here * rows_out, rows_out), rows_out)],
            regrouped_ref.at[:, pl.ds(pl.multiple_of(head * cols, cols), cols)],
            rows_sem.at[head],
        )

    def gram(head):
        rows_copy(head).start()
        owner = lax.div(head, per_group)
        local = lax.rem(head, per_group)
        shift = lax.rem(owner - me + groups, groups)

        def one(t, carry):
            where = pl.ds(pl.multiple_of(t * tile, tile), tile)
            term = lax.dot_general(
                gathered[head, :, where], gathered[here],
                (((0,), (0,)), ((), ())), preferred_element_type=jnp.float32,
            )

            @pl.when(shift == 0)
            def _():
                total[local, where] = term

            @pl.when(shift != 0)
            def _():
                leaving[shift - 1, local, where] = term.astype(jnp.bfloat16)

            return carry

        lax.fori_loop(0, cols // tile, one, 0)

        sends = shift != 0
        if lending:
            sends = sends & jnp.logical_not(borrows & (lax.div(head, 2) == held))

        @pl.when(sends)
        def _():
            sum_copy(shift, local).start()

    def lent_copy(which):
        return pltpu.make_async_remote_copy(
            src_ref=lent.at[which], dst_ref=relayed.at[which],
            send_sem=lent_send.at[which], recv_sem=lent_recv.at[which],
            device_id=(1 - me, here), device_id_type=MESH,
        )

    def relay_copy(which):
        local = lax.rem((level * 2 + 1 - side) * 2 + which, per_group)
        return pltpu.make_async_remote_copy(
            src_ref=relayed.at[which], dst_ref=arrived.at[0, local],
            send_sem=relay_send.at[which], recv_sem=sum_recv.at[0, local],
            device_id=(me, mirror), device_id_type=MESH,
        )

    def gram_for_mirror(which):
        head = (level * 2 + 1 - side) * 2 + which

        def one(t, carry):
            where = pl.ds(pl.multiple_of(t * tile, tile), tile)
            lent[which, where] = lax.dot_general(
                gathered[head, :, where], gathered[mirror],
                (((0,), (0,)), ((), ())), preferred_element_type=jnp.float32,
            ).astype(jnp.bfloat16)
            return carry

        lax.fori_loop(0, cols // tile, one, 0)
        lent_copy(which).start()

    def gram_far(head):
        if not lending:
            gram(head)
            return

        @pl.when(lends)
        def _():
            rows_copy(head).start()

        @pl.when(jnp.logical_not(lends))
        def _():
            gram(head)

    reach = {(0, 0): depth, (1, 0): depth - 1, (0, 1): depth - 1, (1, 1): depth}
    for load in loads:
        load.wait()
    for part in range(2):
        attend(part)
        if part == 0:
            pl.semaphore_wait(barrier, 3 + groups - 1 + int(lending))
        for direction in range(2):
            ring(direction, part, 0).start()
        pair(0, part, 0, core).start()
    gram(here)

    def receive(part, step):
        for direction in range(2):
            ring_arrival(direction, part, step).wait_recv()
            if reach[direction, part] == depth:
                ring(direction, part, step).start()
            else:
                @pl.when(step < depth - 1)
                def _():
                    ring(direction, part, step).start()
            pair(direction, part, step, core).start()

    def pair_arrivals(step):
        for part in range(2):
            for direction in range(2):
                pair(direction, part, step, 1 - core).wait_recv()

    def advance(step, carry):
        receive(0, step)

        @pl.when(step == 1)
        def _():
            for part in range(2):
                pair(0, part, 0, 1 - core).wait_recv()
            gram(partner)

        @pl.when(step > 1)
        def _():
            pair_arrivals(step - 1)
            gram(head_at(place - step + 1, 1 - core))
            gram(head_at(place + step - 1, 1 - core))

        receive(1, step)
        if lending:
            @pl.when(borrows & (step == depth - 1))
            def _():
                for which in range(2):
                    gram_for_mirror(which)
                for which in range(2):
                    sum_copy(1, lax.rem(held * 2 + which, per_group)).start()

        gram(head_at(place - step, core))
        gram(head_at(place + step, core))
        return carry

    lax.fori_loop(1, depth, advance, 0)
    for direction, part in ((0, 0), (1, 1)):
        ring_arrival(direction, part, depth).wait_recv()
        pair(direction, part, depth, core).start()
    if depth > 1:
        pair_arrivals(depth - 1)
        gram(head_at(place - depth + 1, 1 - core))
        gram(head_at(place + depth - 1, 1 - core))
    gram_far(head_at(place - depth, core))
    for direction, part in ((0, 0), (1, 1)):
        pair(direction, part, depth, 1 - core).wait_recv()
    gram_far(head_at(place - depth, 1 - core))

    def finish(order, carry):
        if lending:
            @pl.when(lends & (order == 4))
            def _():
                for which in range(2):
                    lent_copy(which).wait_recv()
                    relay_copy(which).start()

        away = lax.div(order, 4)
        kind = lax.rem(order, 4)
        head = head_at(
            place + (away + 1) * (2 * lax.rem(kind, 2) - 1), lax.rem(core + lax.div(kind, 2), 2)
        )
        collect(head)
        return carry

    def collect(head):
        owner = lax.div(head, per_group)
        local = lax.rem(head, per_group)

        @pl.when(owner == me)
        def _():
            for shift in range(1, groups):
                sum_copy(shift, local).wait_recv()
            value = total[local]
            for shift in range(1, groups):
                value = value + arrived[shift - 1, local].astype(jnp.float32)
            total[local] = value * scale

    collect(here)
    collect(partner)
    lax.fori_loop(0, 4 * (depth - 1), finish, 0)
    collect(head_at(place - depth, core))
    collect(head_at(place - depth, 1 - core))

    if lending:
        @pl.when(lends)
        def _():
            for which in range(2):
                relay_copy(which).wait_send()

    def drain(head, carry):
        rows_copy(head).wait()
        owner = lax.div(head, per_group)
        local = lax.rem(head, per_group)
        shift = lax.rem(owner - me + groups, groups)

        sends = shift != 0
        if lending:
            lent_out = lends & (lax.div(head, 2) == (layers - 1 - level) * 2 + 1 - side)
            sends = sends & jnp.logical_not(lent_out)

        @pl.when(sends)
        def _():
            sum_copy(shift, local).wait_send()

        return carry

    lax.fori_loop(0, heads, drain, 0)

    def drain_sends(step, carry):
        for (direction, part), distance in reach.items():
            @pl.when(step < distance)
            def _():
                ring(direction, part, step).wait_send()

            @pl.when((step > 0) & (step <= distance))
            def _():
                pair(direction, part, step, core).wait_send()
        return carry

    lax.fori_loop(0, depth + 1, drain_sends, 0)
    for part in range(2):
        pair(0, part, 0, core).wait_send()
    if lending:
        @pl.when(borrows)
        def _():
            for which in range(2):
                lent_copy(which).wait_send()


def exchange(queries, keys, values, groups, heads):
    rows, cols = queries.shape
    per_group = heads // groups
    depth = heads // 4
    dma = pltpu.SemaphoreType.DMA
    vmem = pl.BlockSpec(memory_space=pltpu.VMEM)
    return pl.pallas_call(
        functools.partial(exchange_kernel, groups, heads, 2.0 / (rows * groups)),
        out_shape=(
            pltpu.VMEM((rows // heads, heads * cols), jnp.bfloat16),
            pltpu.VMEM((per_group, cols, cols), jnp.float32),
        ),
        in_specs=[pl.BlockSpec(memory_space=pltpu.HBM)] * 3,
        out_specs=(vmem, vmem),
        scratch_shapes=[
            pltpu.VMEM((rows, cols), jnp.bfloat16),
            pltpu.VMEM((rows, cols), jnp.bfloat16),
            pltpu.VMEM((rows, cols), jnp.bfloat16),
            pltpu.VMEM((heads, rows, cols), jnp.bfloat16),
            pltpu.VMEM((groups - 1, per_group, cols, cols), jnp.bfloat16),
            pltpu.VMEM((groups - 1, per_group, cols, cols), jnp.bfloat16),
            pltpu.VMEM((2, cols, cols), jnp.bfloat16),
            pltpu.VMEM((2, cols, cols), jnp.bfloat16),
            dma((2, 2, depth)),
            dma((2, 2, depth)),
            dma((2, 2, depth + 1)),
            dma((2, 2, depth + 1)),
            dma((groups - 1, per_group)),
            dma((groups - 1, per_group)),
            dma((heads,)),
            dma((3,)),
            dma((2,)),
            dma((2,)),
            dma((2,)),
        ],
        compiler_params=pltpu.CompilerParams(
            collective_id=0, has_side_effects=True, vmem_limit_bytes=109 * 512 * 1024
        ),
    )(queries, keys, values)


LAYERS = 4
RECV, SEND, GRAM, ROWS, HELD, MAKE, TAKE, IDLE = range(8)
OPS = (
    (
        14848, 14976, 8448, 8576, 33282, 33410, 49666, 49794, 769, 2305, 4353, 8200, 8208, 8256, 33290,
        33298, 770, 898, 17154, 49674, 49682, 897, 2433, 4481, 17282, 8328, 8464, 8384, 33418, 786, 66, 194,
        16450, 49802, 17170, 4113, 16578, 8456, 34848, 8776, 778, 74, 17162, 16458, 4369, 8584, 34976, 8904,
        906, 202, 17290, 16586, 4129, 905, 8216, 35104, 8512, 33306, 49690, 4257, 8984, 35232, 8648, 4643,
        794, 17178, 521, 34856, 12432, 8640, 33426, 322, 450, 16706, 458, 16842, 16420, 49810, 16834, 34984,
        12688, 8520, 914, 330, 17298, 16714, 4385, 8344, 35000, 8272, 33434, 82, 49818, 16466, 4513, 8600,
        35256, 8528, 922, 338, 17306, 16722, 35112, 12504, 32824, 218, 16602, 35240, 12760, 70187, 132139,
        201771, 474, 16858, 8400, 8536, 210, 346, 33080, 266811, 330299, 399931, 16428, 16594, 16730, 8656,
        8280, 466, 90, 16850, 16474, 16444, 52, 16436,
    ),
    (
        15888, 14992, 9488, 10640, 33298, 33426, 49682, 49810, 785, 8192, 8216, 33824, 12368, 33282, 33306,
        786, 914, 17170, 49666, 49690, 913, 17298, 12416, 8344, 36000, 8528, 33410, 33434, 49794, 49818,
        12544, 8280, 36128, 8768, 770, 17154, 4433, 8576, 8840, 36256, 8512, 4643, 898, 33418, 17282, 49802,
        1169, 4497, 10312, 8968, 33080, 8520, 33546, 16420, 49930, 1425, 833, 2361, 12488, 8536, 8400, 8640,
        66, 16450, 74, 202, 16458, 82, 210, 16466, 90, 16474, 16586, 16594, 9096, 8600, 36024, 12752, 906,
        922, 322, 450, 16706, 16834, 330, 16714, 338, 466, 16722, 346, 961, 16730, 17290, 17306, 16850,
        8472, 8384, 36280, 8648, 794, 194, 458, 17178, 16578, 2321, 16842, 8712, 8664, 9432, 522, 218, 474,
        16906, 16602, 705, 1497, 16858, 34872, 70203, 133691, 203323, 1369, 1113, 16444, 52, 16436, 44,
        16428,
    ),
    (
        3616, 1184, 2848, 416, 1313, 8720, 96, 34864, 33298, 4643, 68131, 137763, 197667, 267299, 330787,
        400419, 49682, 1441, 8848, 224, 39216, 33426, 16420, 49810, 13072, 480, 32944, 786, 44, 16428,
        36152, 17170, 9104, 13520, 35248, 463411, 914, 210, 8472, 33562, 17298, 16594, 2465, 49946, 8768,
        12624, 33976, 32834, 8408, 32986, 16436, 49218, 49370, 8840, 12752, 36280, 33418, 8536, 49802, 1241,
        13064, 32824, 12368, 528955, 33546, 82, 8664, 49930, 16466, 1081, 9024, 8520, 8344, 666, 8448, 770,
        16444, 17050, 17154, 13192, 8392, 8216, 906, 538, 202, 8280, 90, 17290, 16922, 16586, 16474, 9152,
        8648, 8600, 922, 8576, 33666, 17306, 50050, 12808, 352, 522, 322, 450, 16706, 16834, 330, 458,
        16714, 8320, 16842, 338, 466, 16722, 16850, 346, 474, 16730, 16858, 642, 16906, 17026, 8384, 8264,
        194, 74, 8704, 514, 16578, 16458, 16898,
    ),
    (
        7216, 6320, 1328, 432, 1201, 4401, 112, 32, 34872, 4659, 1457, 4529, 240, 288, 35000, 2353, 1209,
        16436, 368, 12304, 33080, 33298, 49682, 496, 12432, 36280, 70203, 33426, 49810, 2481, 9296, 12560,
        8216, 786, 33306, 82, 16444, 17170, 2361, 49690, 16466, 8400, 12688, 9368, 914, 33434, 210, 17298,
        49818, 2081, 1049, 16594, 8528, 12352, 8472, 794, 32834, 338, 17178, 49218, 2337, 16722, 8656,
        12424, 9624, 33418, 922, 466, 49802, 17306, 16850, 8280, 12552, 10312, 33546, 74, 90, 49930, 16458,
        16474, 8408, 12608, 9344, 33410, 322, 218, 49794, 16706, 16602, 12488, 8584, 8448, 770, 906, 202,
        17154, 17290, 4489, 16586, 8648, 8640, 10568, 450, 330, 458, 16834, 16714, 16842, 8536, 8200, 8384,
        522, 194, 346, 16906, 16578, 16730, 8664, 8192, 8576, 514, 898, 474, 16898, 17282, 16858, 36, 16420,
        44, 16428,
    ),
)
MADE = 8


def routed_kernel(
    heads, scale,
    query_hbm, key_hbm, value_hbm, regrouped_ref, total,
    query_ref, key_ref, value_ref, store, made, taken, landed,
    recv_sem, send_sem, made_sem, take_sem, rows_send, rows_recv, load_sem,
):
    rows, cols = query_ref.shape
    quarter = rows // 4
    half = rows // 2
    wide = cols // 2
    rows_out = rows // heads
    layer = heads // LAYERS
    me = lax.axis_index("dp")
    here = lax.axis_index("head")
    core = lax.rem(here, 2)
    chip = lax.div(here, 2)
    side = lax.rem(chip, 2)
    level = lax.div(chip, 2)
    role = level + me * (LAYERS - 1 - 2 * level)
    up = (1 - 2 * me) * layer
    across = 2 - 4 * side
    cross = 1 - 2 * core
    mine = (me * heads + here) * 4
    channels = {
        0: (me, here + up), 1: (me, here - up), 2: (1 - me, here),
        3: (me, here + across), 4: (me, here + cross),
    }

    loads = []
    for strip in range(4):
        part = pl.ds(strip * quarter, quarter)
        group = [
            pltpu.make_async_copy(source.at[part], target.at[part], load_sem.at[strip * 3 + n])
            for n, (source, target) in enumerate(
                ((query_hbm, query_ref), (key_hbm, key_ref), (value_hbm, value_ref))
            )
        ]
        for load in group:
            load.start()
        loads.append(group)

    barrier = pltpu.get_barrier_semaphore()
    for rise in (-1, 0, 1):
        @pl.when((role + rise >= 0) & (role + rise < LAYERS))
        def _():
            for turn in range(2):
                for swap in range(2):
                    if (rise, turn, swap) == (0, 0, 0):
                        continue
                    there = here + rise * up + turn * across + swap * cross
                    pl.semaphore_signal(barrier, inc=1, device_id=(me, there), device_id_type=MESH)
    pl.semaphore_signal(barrier, inc=1, device_id=(1 - me, here), device_id_type=MESH)
    ends = lax.rem(lax.div(role + 1, 2) + 1, 2)

    def base_of(block):
        other = lax.div(block, 8)
        height = lax.rem(lax.div(block, 2), 4)
        turn = lax.rem(block, 2)
        sequence = me + other - 2 * me * other
        floor = height + me * (LAYERS - 1 - 2 * height)
        spot = floor * 2 + side + turn - 2 * side * turn
        return (sequence * heads + spot * 2 + core) * 4

    length = max(len(ops) for ops in OPS)

    def pick(index):
        words = [ops[index] if index < len(ops) else IDLE for ops in OPS]
        low = jnp.where(role == 0, words[0], words[1])
        high = jnp.where(role == 2, words[2], words[3])
        return jnp.where(role < 2, low, high)

    def word_at(index, first, last):
        if last - first == 1:
            return pick(first)
        middle = (first + last) // 2
        return lax.cond(
            index < middle, lambda: word_at(index, first, middle), lambda: word_at(index, middle, last)
        )

    def copy(channel, slot):
        return pltpu.make_async_remote_copy(
            src_ref=store.at[slot], dst_ref=store.at[slot],
            send_sem=send_sem.at[channel], recv_sem=recv_sem.at[slot],
            device_id=channels[channel], device_id_type=MESH,
        )

    def send(mask, slot):
        for channel in range(5):
            @pl.when(lax.rem(lax.div(mask, 2 ** channel), 2) == 1)
            def _():
                copy(channel, slot).start()

    def head_of(slot):
        return lax.rem(lax.div(slot, 4), heads)

    def columns(head, pair):
        return pl.ds(pl.multiple_of(head * cols + pair * wide, wide), wide)

    def keep_rows(slot):
        first = here * rows_out - lax.rem(lax.div(slot, 2), 2) * half

        @pl.when((first >= 0) & (first < half))
        def _():
            regrouped_ref[:, columns(head_of(slot), lax.rem(slot, 2))] = store[
                slot, pl.ds(pl.multiple_of(first, rows_out), rows_out)
            ]

    def rows_copy(base, mask, number, pair):
        there = here + (lax.rem(mask, 4) - 1) * up + lax.rem(lax.div(mask, 4), 2) * across
        there = there + lax.div(mask, 8) * cross
        late = lax.div(there * rows_out, half)
        return pltpu.make_async_remote_copy(
            src_ref=store.at[
                base + late * 2 + pair,
                pl.ds(pl.multiple_of(there * rows_out - late * half, rows_out), rows_out),
            ],
            dst_ref=landed.at[head_of(base) * 2 + pair],
            send_sem=rows_send.at[number * 2 + pair], recv_sem=rows_recv.at[head_of(base) * 2 + pair],
            device_id=(me, there), device_id_type=MESH,
        )

    def take_copy(channel, number):
        return pltpu.make_async_remote_copy(
            src_ref=made.at[number], dst_ref=taken.at[number],
            send_sem=made_sem.at[number], recv_sem=take_sem.at[number],
            device_id=channels[channel], device_id_type=MESH,
        )

    def local_rows(slot, pair):
        return pl.ds(pl.multiple_of((head_of(slot) - me * (heads // 2)) * cols + pair * wide, wide), wide)

    def term(left, right):
        return lax.dot_general(
            store[left], store[right], (((0,), (0,)), ((), ())), preferred_element_type=jnp.float32,
        )

    def attend(strip, pair):
        seen = (strip + 1) * quarter
        here_rows = pl.ds(strip * quarter, quarter)
        for inner in range(wide // HEAD_SIZE):
            lanes = pl.ds(pl.multiple_of(pair * wide + inner * HEAD_SIZE, HEAD_SIZE), HEAD_SIZE)
            logits = lax.dot_general(
                query_ref[here_rows, lanes], key_ref[pl.ds(0, seen), lanes],
                (((1,), (1,)), ((), ())), preferred_element_type=jnp.float32,
            ) * (1.0 / math.sqrt(HEAD_SIZE))
            corner = logits[:, strip * quarter:]
            row = lax.broadcasted_iota(jnp.int32, corner.shape, 0)
            column = lax.broadcasted_iota(jnp.int32, corner.shape, 1)
            corner = jnp.where(row >= column, corner, -1e30)
            logits = jnp.concatenate([logits[:, :strip * quarter], corner], axis=1) if strip else corner
            raised = jnp.exp(logits - jnp.max(logits, axis=-1, keepdims=True))
            weight = raised * (1.0 / jnp.sum(raised, axis=-1, keepdims=True))
            store[
                mine + strip // 2 * 2 + pair, pl.ds(strip % 2 * quarter, quarter),
                pl.ds(inner * HEAD_SIZE, HEAD_SIZE),
            ] = jnp.dot(
                weight.astype(jnp.bfloat16), value_ref[pl.ds(0, seen), lanes],
                preferred_element_type=jnp.float32,
            ).astype(jnp.bfloat16)

    for part in range(2):
        for strip in (2 * part, 2 * part + 1):
            for load in loads[strip]:
                load.wait()

        def of_pair(pair, carry):
            for strip in (2 * part, 2 * part + 1):
                attend(strip, pair)
            if part == 0:
                @pl.when(pair == 0)
                def _():
                    pl.semaphore_wait(barrier, 3 * layer - ends * layer)
            piece = part * 2 + pair
            send(lax.rem(lax.div(word_at(piece, 0, 4), 512), 32), mine + piece)
            keep_rows(mine + piece)
            return carry

        lax.fori_loop(0, 2, of_pair, 0)

    def step(index, carry):
        word = word_at(index, 4, length)
        kind = lax.rem(word, 8)
        base = base_of(lax.rem(lax.div(word, 8), 16))
        piece = lax.rem(lax.div(word, 128), 4)
        mask = lax.rem(lax.div(word, 512), 32)
        lane = lax.rem(lax.div(word, 16384), 2)
        flag = lax.rem(lax.div(word, 32768), 2)
        number = lax.div(word, 65536)
        base = base + lane * cross * 4
        slot = base + piece

        @pl.when(kind <= SEND)
        def _():
            @pl.when(kind == RECV)
            def _():
                copy(4, slot).wait_recv()
            send(mask, slot)

            @pl.when(flag == 1)
            def _():
                keep_rows(slot)

        @pl.when(kind == GRAM)
        def _():
            @pl.when(lane == 1)
            def _():
                copy(4, slot).wait_recv()
            own = (lax.div(slot, heads * 4) * heads + here) * 4 + lax.div(piece, 2) * 2
            target = local_rows(slot, lax.rem(piece, 2))
            for other in range(2):
                lanes = pl.ds(other * wide, wide)
                total[target, lanes] = (
                    jnp.where(flag == 1, 0.0, total[target, lanes]) + term(slot, own + other) * scale
                )

            @pl.when(mask == 1)
            def _():
                keep_rows(slot)

        @pl.when((kind > GRAM) & (kind != IDLE))
        def _():
            @pl.when(kind == ROWS)
            def _():
                for pair in range(2):
                    rows_copy(base, mask, number, pair).start()

            @pl.when(kind == HELD)
            def _():
                for pair in range(2):
                    pltpu.make_async_remote_copy(
                        src_ref=store.at[base, pl.ds(0, rows_out)],
                        dst_ref=landed.at[head_of(base) * 2 + pair],
                        send_sem=rows_send.at[pair], recv_sem=rows_recv.at[head_of(base) * 2 + pair],
                        device_id=channels[4], device_id_type=MESH,
                    ).wait_recv()
                    regrouped_ref[:, columns(head_of(base), pair)] = landed[head_of(base) * 2 + pair]

            @pl.when(kind == MAKE)
            def _():
                column = base_of(lax.div(number, 16))
                far = lax.rem(base + 4 * heads, 8 * heads)
                column_far = lax.rem(column + 4 * heads, 8 * heads)
                for other in range(2):
                    value = jnp.zeros((wide, wide), jnp.float32)
                    for left, right in ((base, column), (far, column_far)):
                        for part in range(2):
                            value = value + term(left + part * 2 + piece, right + part * 2 + other)
                    made[lax.rem(number, 16), :, other * wide:(other + 1) * wide] = value.astype(jnp.bfloat16)
                for channel in range(4):
                    @pl.when(lax.rem(lax.div(mask, 2 ** channel), 2) == 1)
                    def _():
                        take_copy(channel, lax.rem(number, 16)).start()

            @pl.when(kind == TAKE)
            def _():
                take_copy(0, number).wait_recv()
                total[local_rows(base, piece), :] = taken[number].astype(jnp.float32) * scale

        return carry

    lax.fori_loop(4, length, step, 0)

    for which, ops in enumerate(OPS):
        @pl.when(role == which)
        def _():
            for channel in range(5):
                count = sum(word & 7 <= SEND and word >> 9 + channel & 1 for word in ops)
                if count:
                    sent = store.at[pl.ds(0, count)]
                    pltpu.make_async_remote_copy(
                        src_ref=sent, dst_ref=sent, send_sem=send_sem.at[channel],
                        recv_sem=recv_sem.at[0], device_id=channels[4], device_id_type=MESH,
                    ).wait_send()
            for word in ops:
                if word & 7 == ROWS:
                    for pair in range(2):
                        rows_copy(base_of(word >> 3 & 15), word >> 9 & 31, word >> 16, pair).wait_send()
                if word & 7 == MAKE:
                    take_copy(4, word >> 16 & 15).wait_send()


def routed(queries, keys, values, groups, heads):
    rows, cols = queries.shape
    dma = pltpu.SemaphoreType.DMA
    vmem = pl.BlockSpec(memory_space=pltpu.VMEM)
    shard = pltpu.VMEM((rows, cols), jnp.bfloat16)
    strip = pltpu.VMEM((MADE, cols // 2, cols), jnp.bfloat16)
    return pl.pallas_call(
        functools.partial(routed_kernel, heads, 2.0 / (rows * groups)),
        out_shape=(
            pltpu.VMEM((rows // heads, heads * cols), jnp.bfloat16),
            pltpu.VMEM((heads // groups * cols, cols), jnp.float32),
        ),
        in_specs=[pl.BlockSpec(memory_space=pltpu.HBM)] * 3,
        out_specs=(vmem, vmem),
        scratch_shapes=[
            shard, shard, shard,
            pltpu.VMEM((groups * heads * 4, rows // 2, cols // 2), jnp.bfloat16),
            strip, strip,
            pltpu.VMEM((heads * 2, rows // heads, cols // 2), jnp.bfloat16),
            dma((groups * heads * 4,)),
            dma((5,)),
            dma((MADE,)),
            dma((MADE,)),
            dma((heads * 2,)),
            dma((heads * 2,)),
            dma((12,)),
        ],
        compiler_params=pltpu.CompilerParams(
            collective_id=0, has_side_effects=True, vmem_limit_bytes=109 * 512 * 1024
        ),
    )(queries, keys, values)


def body(queries, keys, values):
    cols = queries.shape[1]
    groups, heads = lax.axis_size("dp"), lax.axis_size("head")
    fits = groups == 2 and heads == 4 * LAYERS and cols % (4 * HEAD_SIZE) == 0
    regrouped, total = (routed if fits else exchange)(queries, keys, values, groups, heads)
    return (regrouped, total.reshape(-1, cols))


def solution(mesh):
    in_specs = (P("dp", "head"), P("dp", "head"), P("dp", "head"))
    out_specs = (P(("dp", "head"), None), P("dp", "head"))
    return jax.shard_map(body, mesh=mesh, in_specs=in_specs, out_specs=out_specs, check_vma=False)
```

```python
import functools
import math

import jax
import jax.numpy as jnp
from jax import lax
from jax.experimental import pallas as pl
from jax.experimental.pallas import tpu as pltpu
from jax.sharding import PartitionSpec as P

HEAD_SIZE = 128
MESH = pl.DeviceIdType.MESH


def exchange_kernel(
    groups, heads, scale,
    query_hbm, key_hbm, value_hbm, regrouped_ref, total,
    query_ref, key_ref, value_ref, gathered, leaving, arrived, lent, relayed,
    ring_send, ring_recv, pair_send, pair_recv, sum_send, sum_recv,
    rows_sem, load_sem, lent_send, lent_recv, relay_send,
):
    rows, cols = query_ref.shape
    half = rows // 2
    quarter = rows // 4
    chips = heads // 2
    depth = chips // 2
    per_group = heads // groups
    rows_out = rows // heads
    tile = min(cols, 256)
    me = lax.axis_index("dp")
    here = lax.axis_index("head")
    core = lax.rem(here, 2)
    chip = lax.div(here, 2)
    layers = chips // 2
    side = lax.rem(chip, 2)
    level = lax.div(chip, 2)
    place = level + side * (2 * layers - 1 - 2 * level)

    def head_at(position, which):
        spot = lax.rem(position + 2 * chips, chips)
        far = lax.div(spot, layers)
        height = spot + far * (2 * layers - 1 - 2 * spot)
        return (height * 2 + far) * 2 + which

    right = head_at(place + 1, core)
    left = head_at(place - 1, core)
    partner = here + 1 - 2 * core

    loads = [
        pltpu.make_async_copy(source, target, load_sem.at[n])
        for n, (source, target) in enumerate(
            ((query_hbm, query_ref), (key_hbm, key_ref), (value_hbm, value_ref))
        )
    ]
    for load in loads:
        load.start()
    lending = groups == 2 and layers >= 4
    lends = level == (layers - 1) * me
    borrows = level == (layers - 1) * (1 - me)
    held = (level + 2 * me - 1) * 2 + 1 - side
    mirror = ((layers - 1 - level) * 2 + side) * 2 + core

    barrier = pltpu.get_barrier_semaphore()
    if lending:
        pl.semaphore_signal(barrier, inc=1, device_id=(me, mirror), device_id_type=MESH)
    for other in (right, left, partner):
        pl.semaphore_signal(barrier, inc=1, device_id=(me, other), device_id_type=MESH)
    for shift in range(1, groups):
        pl.semaphore_signal(
            barrier, inc=1, device_id=(lax.rem(me + shift, groups), here), device_id_type=MESH
        )

    def attend(part):
        def head_of(index, carry):
            lanes = pl.ds(pl.multiple_of(index * HEAD_SIZE, HEAD_SIZE), HEAD_SIZE)
            for strip in range(2 * part, 2 * part + 2):
                seen = (strip + 1) * quarter
                here_rows = pl.ds(strip * quarter, quarter)
                logits = lax.dot_general(
                    query_ref[here_rows, lanes], key_ref[pl.ds(0, seen), lanes],
                    (((1,), (1,)), ((), ())), preferred_element_type=jnp.float32,
                ) * (1.0 / math.sqrt(HEAD_SIZE))
                row = lax.broadcasted_iota(jnp.int32, logits.shape, 0) + strip * quarter
                column = lax.broadcasted_iota(jnp.int32, logits.shape, 1)
                logits = jnp.where(row >= column, logits, -1e30)
                raised = jnp.exp(logits - jnp.max(logits, axis=-1, keepdims=True))
                weight = raised * (1.0 / jnp.sum(raised, axis=-1, keepdims=True))
                gathered[here, here_rows, lanes] = jnp.dot(
                    weight.astype(jnp.bfloat16), value_ref[pl.ds(0, seen), lanes],
                    preferred_element_type=jnp.float32,
                ).astype(jnp.bfloat16)
            return carry

        lax.fori_loop(0, cols // HEAD_SIZE, head_of, 0)

    def block(head, part):
        return gathered.at[head, pl.ds(part * half, half)]

    def ring(direction, part, step):
        source = head_at(place + step * (2 * direction - 1), core)
        ref = block(source, part)
        return pltpu.make_async_remote_copy(
            src_ref=ref, dst_ref=ref,
            send_sem=ring_send.at[direction, part, step],
            recv_sem=ring_recv.at[direction, part, step],
            device_id=(me, right if direction == 0 else left), device_id_type=MESH,
        )

    def ring_arrival(direction, part, step):
        source = head_at(place + step * (2 * direction - 1), core)
        ref = block(source, part)
        return pltpu.make_async_remote_copy(
            src_ref=ref, dst_ref=ref,
            send_sem=ring_send.at[direction, part, step - 1],
            recv_sem=ring_recv.at[direction, part, step - 1],
            device_id=(me, right if direction == 0 else left), device_id_type=MESH,
        )

    def pair(direction, part, step, which):
        ref = block(head_at(place + step * (2 * direction - 1), which), part)
        return pltpu.make_async_remote_copy(
            src_ref=ref, dst_ref=ref,
            send_sem=pair_send.at[direction, part, step],
            recv_sem=pair_recv.at[direction, part, step],
            device_id=(me, partner), device_id_type=MESH,
        )

    def sum_copy(shift, local):
        return pltpu.make_async_remote_copy(
            src_ref=leaving.at[shift - 1, local], dst_ref=arrived.at[shift - 1, local],
            send_sem=sum_send.at[shift - 1, local], recv_sem=sum_recv.at[shift - 1, local],
            device_id=(lax.rem(me + shift, groups), here), device_id_type=MESH,
        )

    def rows_copy(head):
        return pltpu.make_async_copy(
            gathered.at[head, pl.ds(pl.multiple_of(here * rows_out, rows_out), rows_out)],
            regrouped_ref.at[:, pl.ds(pl.multiple_of(head * cols, cols), cols)],
            rows_sem.at[head],
        )

    def gram(head):
        rows_copy(head).start()
        owner = lax.div(head, per_group)
        local = lax.rem(head, per_group)
        shift = lax.rem(owner - me + groups, groups)

        def one(t, carry):
            where = pl.ds(pl.multiple_of(t * tile, tile), tile)
            term = lax.dot_general(
                gathered[head, :, where], gathered[here],
                (((0,), (0,)), ((), ())), preferred_element_type=jnp.float32,
            )

            @pl.when(shift == 0)
            def _():
                total[local, where] = term

            @pl.when(shift != 0)
            def _():
                leaving[shift - 1, local, where] = term.astype(jnp.bfloat16)

            return carry

        lax.fori_loop(0, cols // tile, one, 0)

        sends = shift != 0
        if lending:
            sends = sends & jnp.logical_not(borrows & (lax.div(head, 2) == held))

        @pl.when(sends)
        def _():
            sum_copy(shift, local).start()

    def lent_copy(which):
        return pltpu.make_async_remote_copy(
            src_ref=lent.at[which], dst_ref=relayed.at[which],
            send_sem=lent_send.at[which], recv_sem=lent_recv.at[which],
            device_id=(1 - me, here), device_id_type=MESH,
        )

    def relay_copy(which):
        local = lax.rem((level * 2 + 1 - side) * 2 + which, per_group)
        return pltpu.make_async_remote_copy(
            src_ref=relayed.at[which], dst_ref=arrived.at[0, local],
            send_sem=relay_send.at[which], recv_sem=sum_recv.at[0, local],
            device_id=(me, mirror), device_id_type=MESH,
        )

    def gram_for_mirror(which):
        head = (level * 2 + 1 - side) * 2 + which

        def one(t, carry):
            where = pl.ds(pl.multiple_of(t * tile, tile), tile)
            lent[which, where] = lax.dot_general(
                gathered[head, :, where], gathered[mirror],
                (((0,), (0,)), ((), ())), preferred_element_type=jnp.float32,
            ).astype(jnp.bfloat16)
            return carry

        lax.fori_loop(0, cols // tile, one, 0)
        lent_copy(which).start()

    def gram_far(head):
        if not lending:
            gram(head)
            return

        @pl.when(lends)
        def _():
            rows_copy(head).start()

        @pl.when(jnp.logical_not(lends))
        def _():
            gram(head)

    reach = {(0, 0): depth, (1, 0): depth - 1, (0, 1): depth - 1, (1, 1): depth}
    for load in loads:
        load.wait()
    for part in range(2):
        attend(part)
        if part == 0:
            pl.semaphore_wait(barrier, 3 + groups - 1 + int(lending))
        for direction in range(2):
            ring(direction, part, 0).start()
        pair(0, part, 0, core).start()
    gram(here)

    def receive(part, step):
        for direction in range(2):
            ring_arrival(direction, part, step).wait_recv()
            if reach[direction, part] == depth:
                ring(direction, part, step).start()
            else:
                @pl.when(step < depth - 1)
                def _():
                    ring(direction, part, step).start()
            pair(direction, part, step, core).start()

    def pair_arrivals(step):
        for part in range(2):
            for direction in range(2):
                pair(direction, part, step, 1 - core).wait_recv()

    def advance(step, carry):
        receive(0, step)

        @pl.when(step == 1)
        def _():
            for part in range(2):
                pair(0, part, 0, 1 - core).wait_recv()
            gram(partner)

        @pl.when(step > 1)
        def _():
            pair_arrivals(step - 1)
            gram(head_at(place - step + 1, 1 - core))
            gram(head_at(place + step - 1, 1 - core))

        receive(1, step)
        if lending:
            @pl.when(borrows & (step == depth - 1))
            def _():
                for which in range(2):
                    gram_for_mirror(which)
                for which in range(2):
                    sum_copy(1, lax.rem(held * 2 + which, per_group)).start()

        gram(head_at(place - step, core))
        gram(head_at(place + step, core))
        return carry

    lax.fori_loop(1, depth, advance, 0)
    for direction, part in ((0, 0), (1, 1)):
        ring_arrival(direction, part, depth).wait_recv()
        pair(direction, part, depth, core).start()
    if depth > 1:
        pair_arrivals(depth - 1)
        gram(head_at(place - depth + 1, 1 - core))
        gram(head_at(place + depth - 1, 1 - core))
    gram_far(head_at(place - depth, core))
    for direction, part in ((0, 0), (1, 1)):
        pair(direction, part, depth, 1 - core).wait_recv()
    gram_far(head_at(place - depth, 1 - core))

    def finish(order, carry):
        if lending:
            @pl.when(lends & (order == 4))
            def _():
                for which in range(2):
                    lent_copy(which).wait_recv()
                    relay_copy(which).start()

        away = lax.div(order, 4)
        kind = lax.rem(order, 4)
        head = head_at(
            place + (away + 1) * (2 * lax.rem(kind, 2) - 1), lax.rem(core + lax.div(kind, 2), 2)
        )
        collect(head)
        return carry

    def collect(head):
        owner = lax.div(head, per_group)
        local = lax.rem(head, per_group)

        @pl.when(owner == me)
        def _():
            for shift in range(1, groups):
                sum_copy(shift, local).wait_recv()
            value = total[local]
            for shift in range(1, groups):
                value = value + arrived[shift - 1, local].astype(jnp.float32)
            total[local] = value * scale

    collect(here)
    collect(partner)
    lax.fori_loop(0, 4 * (depth - 1), finish, 0)
    collect(head_at(place - depth, core))
    collect(head_at(place - depth, 1 - core))

    if lending:
        @pl.when(lends)
        def _():
            for which in range(2):
                relay_copy(which).wait_send()

    def drain(head, carry):
        rows_copy(head).wait()
        owner = lax.div(head, per_group)
        local = lax.rem(head, per_group)
        shift = lax.rem(owner - me + groups, groups)

        sends = shift != 0
        if lending:
            lent_out = lends & (lax.div(head, 2) == (layers - 1 - level) * 2 + 1 - side)
            sends = sends & jnp.logical_not(lent_out)

        @pl.when(sends)
        def _():
            sum_copy(shift, local).wait_send()

        return carry

    lax.fori_loop(0, heads, drain, 0)

    def drain_sends(step, carry):
        for (direction, part), distance in reach.items():
            @pl.when(step < distance)
            def _():
                ring(direction, part, step).wait_send()

            @pl.when((step > 0) & (step <= distance))
            def _():
                pair(direction, part, step, core).wait_send()
        return carry

    lax.fori_loop(0, depth + 1, drain_sends, 0)
    for part in range(2):
        pair(0, part, 0, core).wait_send()
    if lending:
        @pl.when(borrows)
        def _():
            for which in range(2):
                lent_copy(which).wait_send()


def exchange(queries, keys, values, groups, heads):
    rows, cols = queries.shape
    per_group = heads // groups
    depth = heads // 4
    dma = pltpu.SemaphoreType.DMA
    vmem = pl.BlockSpec(memory_space=pltpu.VMEM)
    return pl.pallas_call(
        functools.partial(exchange_kernel, groups, heads, 2.0 / (rows * groups)),
        out_shape=(
            pltpu.VMEM((rows // heads, heads * cols), jnp.bfloat16),
            pltpu.VMEM((per_group, cols, cols), jnp.float32),
        ),
        in_specs=[pl.BlockSpec(memory_space=pltpu.HBM)] * 3,
        out_specs=(vmem, vmem),
        scratch_shapes=[
            pltpu.VMEM((rows, cols), jnp.bfloat16),
            pltpu.VMEM((rows, cols), jnp.bfloat16),
            pltpu.VMEM((rows, cols), jnp.bfloat16),
            pltpu.VMEM((heads, rows, cols), jnp.bfloat16),
            pltpu.VMEM((groups - 1, per_group, cols, cols), jnp.bfloat16),
            pltpu.VMEM((groups - 1, per_group, cols, cols), jnp.bfloat16),
            pltpu.VMEM((2, cols, cols), jnp.bfloat16),
            pltpu.VMEM((2, cols, cols), jnp.bfloat16),
            dma((2, 2, depth)),
            dma((2, 2, depth)),
            dma((2, 2, depth + 1)),
            dma((2, 2, depth + 1)),
            dma((groups - 1, per_group)),
            dma((groups - 1, per_group)),
            dma((heads,)),
            dma((3,)),
            dma((2,)),
            dma((2,)),
            dma((2,)),
        ],
        compiler_params=pltpu.CompilerParams(
            collective_id=0, has_side_effects=True, vmem_limit_bytes=109 * 512 * 1024
        ),
    )(queries, keys, values)


LAYERS = 4
RECV, SEND, GRAM, ROWS, HELD, MAKE, TAKE, IDLE = range(8)
OPS = (
    (
        14848, 14976, 8448, 9088, 33282, 33410, 49666, 49794, 2305, 8200, 8208, 12352, 33290, 33298, 770,
        898, 17154, 49674, 49682, 769, 2433, 17282, 8328, 12432, 8512, 33418, 33426, 49802, 49810, 8776,
        14416, 8400, 4305, 8344, 34864, 9032, 33434, 49818, 8792, 14672, 8384, 66, 194, 16450, 74, 16458,
        82, 210, 16466, 16594, 32858, 16578, 49242, 4113, 8408, 34992, 8904, 202, 218, 16586, 16602, 4481,
        8536, 35120, 9152, 322, 450, 16706, 330, 16714, 338, 16722, 346, 16834, 16730, 4401, 8216, 35248,
        33056, 4659, 538, 16922, 8584, 14800, 906, 466, 16436, 17290, 4145, 16850, 32800, 33080, 35256,
        2361, 32928, 8664, 12688, 914, 474, 17298, 16858, 33464, 34872, 12560, 70203, 786, 17170, 33184,
        135715, 199203, 268835, 328739, 8600, 8648, 398371, 922, 458, 16444, 17306, 16842, 8472, 8456, 778,
        794, 16420, 17162, 17178, 44, 16428,
    ),
    (
        15888, 11920, 12560, 10640, 33298, 33426, 49682, 49810, 4241, 785, 8192, 8216, 9296, 33282, 33306,
        786, 914, 17170, 160, 49666, 49690, 913, 4497, 17298, 8320, 8472, 8400, 33410, 794, 82, 210, 16466,
        35888, 49794, 17178, 2209, 16594, 8576, 8344, 14160, 898, 33434, 32944, 17282, 49818, 513, 1201,
        12544, 8600, 8408, 770, 922, 218, 35120, 17154, 17306, 593, 4481, 2225, 1329, 16602, 8264, 8536,
        8384, 194, 32842, 8256, 66, 16578, 49226, 16450, 8520, 8456, 9168, 778, 330, 338, 466, 16722, 346,
        16730, 40368, 4659, 17162, 16714, 2321, 641, 4225, 1489, 16850, 8280, 8584, 8664, 33674, 90, 474,
        8512, 322, 50058, 16474, 897, 4401, 16858, 16436, 16706, 8392, 34232, 8648, 202, 458, 16586, 16842,
        1425, 4145, 769, 8200, 522, 44, 8640, 8328, 32, 16428, 650, 450, 16906, 17034, 16834, 1297, 985,
        35128, 1481, 35384, 1289, 32952, 70203, 16444, 36, 16420,
    ),
    (
        6176, 7840, 288, 416, 2337, 4385, 8720, 96, 32808, 33840, 33298, 4643, 49682, 8848, 224, 34984,
        38064, 33426, 16420, 49810, 4513, 2225, 8976, 480, 33064, 34096, 786, 17170, 2465, 9104, 9280,
        32952, 38320, 70195, 914, 32834, 17298, 49218, 9040, 8400, 35240, 33080, 131115, 200747, 266795,
        328747, 398379, 210, 16436, 16594, 12800, 9536, 35256, 8216, 514, 33306, 16428, 16898, 49690, 14928,
        8384, 8344, 721, 33434, 32962, 82, 9224, 33290, 49818, 49346, 16466, 49674, 8656, 12736, 8472, 794,
        8280, 90, 17178, 16474, 12928, 352, 8600, 977, 642, 922, 322, 450, 16706, 16834, 338, 8648, 466,
        16722, 16850, 33226, 17026, 17306, 49610, 12672, 8536, 898, 346, 8328, 650, 17282, 16730, 17034,
        13056, 770, 8392, 202, 9096, 8520, 906, 330, 17154, 16586, 17290, 16714, 8664, 474, 8408, 218, 8968,
        8264, 778, 74, 16858, 16602, 17162, 16458, 32824, 463419, 16444,
    ),
    (
        3120, 5296, 6448, 432, 1329, 112, 4659, 68147, 137779, 34976, 184, 1457, 240, 2360, 12304, 33298,
        2225, 1337, 16436, 49682, 368, 12432, 33426, 2233, 9240, 33306, 60, 16444, 49810, 496, 49690, 12560,
        786, 2481, 9368, 33434, 17170, 32800, 49818, 12688, 914, 9496, 794, 17298, 8256, 32834, 17178,
        14672, 338, 49218, 9624, 922, 16722, 33056, 17306, 12288, 514, 9560, 346, 16898, 12480, 32962,
        16730, 10320, 82, 49346, 8200, 33290, 16466, 8512, 322, 49674, 14544, 4177, 210, 16706, 11464,
        32970, 16594, 8640, 450, 49354, 12416, 642, 16834, 9432, 218, 17026, 33184, 201251, 16602, 14800,
        466, 8280, 90, 16850, 8648, 458, 16474, 8448, 770, 16420, 16842, 8328, 650, 17154, 8520, 330, 17034,
        12680, 906, 16714, 8664, 474, 17290, 8264, 74, 16858, 8456, 778, 16458, 8576, 898, 17162, 17282, 44,
        16428,
    ),
)
MADE = 8


def routed_kernel(
    heads, scale,
    query_hbm, key_hbm, value_hbm, regrouped_ref, total,
    query_ref, key_ref, value_ref, store, made, taken, landed,
    recv_sem, send_sem, made_sem, take_sem, rows_send, rows_recv, load_sem,
):
    rows, cols = query_ref.shape
    quarter = rows // 4
    half = rows // 2
    wide = cols // 2
    rows_out = rows // heads
    layer = heads // LAYERS
    me = lax.axis_index("dp")
    here = lax.axis_index("head")
    core = lax.rem(here, 2)
    chip = lax.div(here, 2)
    side = lax.rem(chip, 2)
    level = lax.div(chip, 2)
    role = level + me * (LAYERS - 1 - 2 * level)
    up = (1 - 2 * me) * layer
    across = 2 - 4 * side
    cross = 1 - 2 * core
    mine = (me * heads + here) * 4
    channels = {
        0: (me, here + up), 1: (me, here - up), 2: (1 - me, here),
        3: (me, here + across), 4: (me, here + cross),
    }

    loads = []
    for strip in range(4):
        part = pl.ds(strip * quarter, quarter)
        group = [
            pltpu.make_async_copy(source.at[part], target.at[part], load_sem.at[strip * 3 + n])
            for n, (source, target) in enumerate(
                ((query_hbm, query_ref), (key_hbm, key_ref), (value_hbm, value_ref))
            )
        ]
        for load in group:
            load.start()
        loads.append(group)

    barrier = pltpu.get_barrier_semaphore()
    for rise in (-1, 0, 1):
        @pl.when((role + rise >= 0) & (role + rise < LAYERS))
        def _():
            for turn in range(2):
                for swap in range(2):
                    if (rise, turn, swap) == (0, 0, 0):
                        continue
                    there = here + rise * up + turn * across + swap * cross
                    pl.semaphore_signal(barrier, inc=1, device_id=(me, there), device_id_type=MESH)
    pl.semaphore_signal(barrier, inc=1, device_id=(1 - me, here), device_id_type=MESH)
    ends = lax.rem(lax.div(role + 1, 2) + 1, 2)

    def base_of(block):
        other = lax.div(block, 8)
        height = lax.rem(lax.div(block, 2), 4)
        turn = lax.rem(block, 2)
        sequence = me + other - 2 * me * other
        floor = height + me * (LAYERS - 1 - 2 * height)
        spot = floor * 2 + side + turn - 2 * side * turn
        return (sequence * heads + spot * 2 + core) * 4

    length = max(len(ops) for ops in OPS)

    def pick(index):
        words = [ops[index] if index < len(ops) else IDLE for ops in OPS]
        low = jnp.where(role == 0, words[0], words[1])
        high = jnp.where(role == 2, words[2], words[3])
        return jnp.where(role < 2, low, high)

    def word_at(index, first, last):
        if last - first == 1:
            return pick(first)
        middle = (first + last) // 2
        return lax.cond(
            index < middle, lambda: word_at(index, first, middle), lambda: word_at(index, middle, last)
        )

    def copy(channel, slot):
        return pltpu.make_async_remote_copy(
            src_ref=store.at[slot], dst_ref=store.at[slot],
            send_sem=send_sem.at[channel], recv_sem=recv_sem.at[slot],
            device_id=channels[channel], device_id_type=MESH,
        )

    def send(mask, slot):
        for channel in range(5):
            @pl.when(lax.rem(lax.div(mask, 2 ** channel), 2) == 1)
            def _():
                copy(channel, slot).start()

    def head_of(slot):
        return lax.rem(lax.div(slot, 4), heads)

    def columns(head, pair):
        return pl.ds(pl.multiple_of(head * cols + pair * wide, wide), wide)

    def keep_rows(slot):
        first = here * rows_out - lax.rem(lax.div(slot, 2), 2) * half

        @pl.when((first >= 0) & (first < half))
        def _():
            regrouped_ref[:, columns(head_of(slot), lax.rem(slot, 2))] = store[
                slot, pl.ds(pl.multiple_of(first, rows_out), rows_out)
            ]

    def rows_copy(base, mask, number, pair):
        there = here + (lax.rem(mask, 4) - 1) * up + lax.rem(lax.div(mask, 4), 2) * across
        there = there + lax.div(mask, 8) * cross
        late = lax.div(there * rows_out, half)
        return pltpu.make_async_remote_copy(
            src_ref=store.at[
                base + late * 2 + pair,
                pl.ds(pl.multiple_of(there * rows_out - late * half, rows_out), rows_out),
            ],
            dst_ref=landed.at[head_of(base) * 2 + pair],
            send_sem=rows_send.at[number * 2 + pair], recv_sem=rows_recv.at[head_of(base) * 2 + pair],
            device_id=(me, there), device_id_type=MESH,
        )

    def take_copy(channel, number):
        return pltpu.make_async_remote_copy(
            src_ref=made.at[number], dst_ref=taken.at[number],
            send_sem=made_sem.at[number], recv_sem=take_sem.at[number],
            device_id=channels[channel], device_id_type=MESH,
        )

    def local_rows(slot, pair):
        return pl.ds(pl.multiple_of((head_of(slot) - me * (heads // 2)) * cols + pair * wide, wide), wide)

    def term(left, right):
        return lax.dot_general(
            store[left], store[right], (((0,), (0,)), ((), ())), preferred_element_type=jnp.float32,
        )

    def attend(strip, pair):
        seen = (strip + 1) * quarter
        here_rows = pl.ds(strip * quarter, quarter)
        for inner in range(wide // HEAD_SIZE):
            lanes = pl.ds(pl.multiple_of(pair * wide + inner * HEAD_SIZE, HEAD_SIZE), HEAD_SIZE)
            logits = lax.dot_general(
                query_ref[here_rows, lanes], key_ref[pl.ds(0, seen), lanes],
                (((1,), (1,)), ((), ())), preferred_element_type=jnp.float32,
            ) * (1.0 / math.sqrt(HEAD_SIZE))
            corner = logits[:, strip * quarter:]
            row = lax.broadcasted_iota(jnp.int32, corner.shape, 0)
            column = lax.broadcasted_iota(jnp.int32, corner.shape, 1)
            corner = jnp.where(row >= column, corner, -1e30)
            logits = jnp.concatenate([logits[:, :strip * quarter], corner], axis=1) if strip else corner
            raised = jnp.exp(logits - jnp.max(logits, axis=-1, keepdims=True))
            weight = raised * (1.0 / jnp.sum(raised, axis=-1, keepdims=True))
            store[
                mine + strip // 2 * 2 + pair, pl.ds(strip % 2 * quarter, quarter),
                pl.ds(inner * HEAD_SIZE, HEAD_SIZE),
            ] = jnp.dot(
                weight.astype(jnp.bfloat16), value_ref[pl.ds(0, seen), lanes],
                preferred_element_type=jnp.float32,
            ).astype(jnp.bfloat16)

    for part in range(2):
        for strip in (2 * part, 2 * part + 1):
            for load in loads[strip]:
                load.wait()

        def of_pair(pair, carry):
            for strip in (2 * part, 2 * part + 1):
                attend(strip, pair)
            if part == 0:
                @pl.when(pair == 0)
                def _():
                    pl.semaphore_wait(barrier, 3 * layer - ends * layer)
            piece = part * 2 + pair
            send(lax.rem(lax.div(word_at(piece, 0, 4), 512), 32), mine + piece)
            keep_rows(mine + piece)
            return carry

        lax.fori_loop(0, 2, of_pair, 0)

    def step(index, carry):
        word = word_at(index, 4, length)
        kind = lax.rem(word, 8)
        base = base_of(lax.rem(lax.div(word, 8), 16))
        piece = lax.rem(lax.div(word, 128), 4)
        mask = lax.rem(lax.div(word, 512), 32)
        lane = lax.rem(lax.div(word, 16384), 2)
        flag = lax.rem(lax.div(word, 32768), 2)
        number = lax.div(word, 65536)
        base = base + lane * cross * 4
        slot = base + piece

        @pl.when(kind <= SEND)
        def _():
            @pl.when(kind == RECV)
            def _():
                copy(4, slot).wait_recv()
            send(mask, slot)

            @pl.when(flag == 1)
            def _():
                keep_rows(slot)

        @pl.when(kind == GRAM)
        def _():
            @pl.when(lane == 1)
            def _():
                copy(4, slot).wait_recv()
            own = (lax.div(slot, heads * 4) * heads + here) * 4 + lax.div(piece, 2) * 2
            target = local_rows(slot, lax.rem(piece, 2))
            for other in range(2):
                lanes = pl.ds(other * wide, wide)
                total[target, lanes] = (
                    jnp.where(flag == 1, 0.0, total[target, lanes]) + term(slot, own + other) * scale
                )

            @pl.when(mask == 1)
            def _():
                keep_rows(slot)

        @pl.when((kind > GRAM) & (kind != IDLE))
        def _():
            @pl.when(kind == ROWS)
            def _():
                for pair in range(2):
                    rows_copy(base, mask, number, pair).start()

            @pl.when(kind == HELD)
            def _():
                for pair in range(2):
                    pltpu.make_async_remote_copy(
                        src_ref=store.at[base, pl.ds(0, rows_out)],
                        dst_ref=landed.at[head_of(base) * 2 + pair],
                        send_sem=rows_send.at[pair], recv_sem=rows_recv.at[head_of(base) * 2 + pair],
                        device_id=channels[4], device_id_type=MESH,
                    ).wait_recv()
                    regrouped_ref[:, columns(head_of(base), pair)] = landed[head_of(base) * 2 + pair]

            @pl.when(kind == MAKE)
            def _():
                column = base_of(lax.div(number, 16))
                far = lax.rem(base + 4 * heads, 8 * heads)
                column_far = lax.rem(column + 4 * heads, 8 * heads)
                for other in range(2):
                    value = jnp.zeros((wide, wide), jnp.float32)
                    for left, right in ((base, column), (far, column_far)):
                        for part in range(2):
                            value = value + term(left + part * 2 + piece, right + part * 2 + other)
                    made[lax.rem(number, 16), :, other * wide:(other + 1) * wide] = value.astype(jnp.bfloat16)
                for channel in range(4):
                    @pl.when(lax.rem(lax.div(mask, 2 ** channel), 2) == 1)
                    def _():
                        take_copy(channel, lax.rem(number, 16)).start()

            @pl.when(kind == TAKE)
            def _():
                take_copy(0, number).wait_recv()
                total[local_rows(base, piece), :] = taken[number].astype(jnp.float32) * scale

        return carry

    lax.fori_loop(4, length, step, 0)

    for which, ops in enumerate(OPS):
        @pl.when(role == which)
        def _():
            for channel in range(5):
                count = sum(word & 7 <= SEND and word >> 9 + channel & 1 for word in ops)
                if count:
                    sent = store.at[pl.ds(0, count)]
                    pltpu.make_async_remote_copy(
                        src_ref=sent, dst_ref=sent, send_sem=send_sem.at[channel],
                        recv_sem=recv_sem.at[0], device_id=channels[4], device_id_type=MESH,
                    ).wait_send()
            for word in ops:
                if word & 7 == ROWS:
                    for pair in range(2):
                        rows_copy(base_of(word >> 3 & 15), word >> 9 & 31, word >> 16, pair).wait_send()
                if word & 7 == MAKE:
                    take_copy(4, word >> 16 & 15).wait_send()


def routed(queries, keys, values, groups, heads):
    rows, cols = queries.shape
    dma = pltpu.SemaphoreType.DMA
    vmem = pl.BlockSpec(memory_space=pltpu.VMEM)
    shard = pltpu.VMEM((rows, cols), jnp.bfloat16)
    strip = pltpu.VMEM((MADE, cols // 2, cols), jnp.bfloat16)
    return pl.pallas_call(
        functools.partial(routed_kernel, heads, 2.0 / (rows * groups)),
        out_shape=(
            pltpu.VMEM((rows // heads, heads * cols), jnp.bfloat16),
            pltpu.VMEM((heads // groups * cols, cols), jnp.float32),
        ),
        in_specs=[pl.BlockSpec(memory_space=pltpu.HBM)] * 3,
        out_specs=(vmem, vmem),
        scratch_shapes=[
            shard, shard, shard,
            pltpu.VMEM((groups * heads * 4, rows // 2, cols // 2), jnp.bfloat16),
            strip, strip,
            pltpu.VMEM((heads * 2, rows // heads, cols // 2), jnp.bfloat16),
            dma((groups * heads * 4,)),
            dma((5,)),
            dma((MADE,)),
            dma((MADE,)),
            dma((heads * 2,)),
            dma((heads * 2,)),
            dma((12,)),
        ],
        compiler_params=pltpu.CompilerParams(
            collective_id=0, has_side_effects=True, vmem_limit_bytes=109 * 512 * 1024
        ),
    )(queries, keys, values)


def body(queries, keys, values):
    cols = queries.shape[1]
    groups, heads = lax.axis_size("dp"), lax.axis_size("head")
    fits = groups == 2 and heads == 4 * LAYERS and cols % (4 * HEAD_SIZE) == 0
    regrouped, total = (routed if fits else exchange)(queries, keys, values, groups, heads)
    return (regrouped, total.reshape(-1, cols))


def solution(mesh):
    in_specs = (P("dp", "head"), P("dp", "head"), P("dp", "head"))
    out_specs = (P(("dp", "head"), None), P("dp", "head"))
    return jax.shard_map(body, mesh=mesh, in_specs=in_specs, out_specs=out_specs, check_vma=False)
```
